128 devices in a mesh: grp: 4 (over z), tile: 32 (over y, x, core).
Axes of the slice: x: 4, y: 4, z: 4, core: 2. Of those that a mesh axis runs over, the one named last changes fastest.
Arguments:
- shot_data: bfloat16 [128, 256, 512], P('grp', 'tile'), may hold values from -6 to 6
- weight_first: bfloat16 [9, 64], replicated, may hold values from -2 to 2
- weight_middle: bfloat16 [1, 9, 64, 64], replicated, may hold values from -0.25 to 0.25
- weight_last: bfloat16 [9, 64], replicated, may hold values from -0.25 to 0.25
- moveout_maps: bfloat16 [8, 512, 512], replicated, may hold values from -0.25 to 0.25
- block_offset: int32 [256], P(('grp', 'tile')), may hold values from 0 to 7
- block_target: int32 [256, 1], P(('grp', 'tile')), may hold values from 0 to 31
Outputs:
- denoised: bfloat16 [128, 256, 512], P('grp', 'tile')
- stacked: float32 [32, 128, 512], P('grp', 'tile')
The draws below stay inside these ranges and needn't reach their ends.
All inputs are finite; a program needn't handle non-finite values.
Results may differ from the reference program's by a relative error of at most 0.0038.
Values may be sent and summed in bfloat16 or wider, within the bound.
No kernel may reach another device: no remote copies, remote signals or barrier semaphores. Data moves between devices by JAX's collectives and lax.ppermute only.
A program may use at most 512 MiB of HBM per device.

```python
import jax
import jax.numpy as jnp
from jax import lax

CH = 64
LAYERS = 3
RD = 8
SH = 32
NT = 512
OB = 8
BLK = 128
SHOTS = 128
RECV = 256
NBLOCKS = 256
MBLK = 32
N_GRP = 4
N_TILE = 32


def with_ends(values, key, low, largest):
    longest = values.shape.index(max(values.shape))
    spots = []
    for shift in (0, 1):
        where = [jax.random.randint(jax.random.fold_in(key, axis), (), 0, length) for axis, length in enumerate(values.shape)]
        where[longest] = (where[longest] + shift) % values.shape[longest]
        spots.append(tuple(where))
    return values.at[spots[0]].set(low).at[spots[1]].set(largest)


def levels(rng, dims, cuts, smallest, high):
    factor_of = 1.0
    for position, blocks in cuts:
        draws = jax.random.uniform(jax.random.fold_in(jax.random.fold_in(rng, 6), position), (blocks,), jnp.float32, smallest / len(cuts), high / len(cuts))
        factor_of = factor_of * jnp.repeat(jnp.exp(draws), dims[position] // blocks).reshape((-1,) + (1,) * (len(dims) - 1 - position))
    return factor_of


def different_ones(key, rows, amount, top, lift):
    sequence = jax.random.permutation(jax.random.fold_in(key, 1), amount)
    favour = sequence
    for power in range(3):
        favour = favour * favour // amount
    favour = favour * lift // amount
    lots = jax.random.randint(jax.random.fold_in(key, 2), (rows, amount), 0, 4096) + favour
    holders = jax.random.permutation(jax.random.fold_in(key, 3), rows)[jnp.arange(amount) % rows]
    lots = jnp.where(jnp.arange(rows)[:, None] == holders[None, :], 1 << 14, lots)
    score = lots * amount + jnp.arange(amount)
    return lax.top_k(score.astype(jnp.int32), top)[1].astype(jnp.int32)


def gaussian(stream_key, shape, deviation, most, cuts=(), kind=jnp.bfloat16):
    factor_of = levels(stream_key, shape, cuts, -0.22, 0.18) if cuts else 1.0
    values = jax.random.normal(stream_key, shape, jnp.float32) * deviation * factor_of
    return jnp.minimum(jnp.maximum(values, -most), most).astype(kind)


def setup_inputs(seed: int = 0) -> dict:
    splits = jax.random.split(jax.random.key(seed), 8)
    return {
        "shot_data": gaussian(splits[0], (SHOTS, RECV, NT), 1.0, 6.0, ((0, 4), (1, 32))),
        "weight_first": gaussian(splits[1], (9, CH), 9 ** -0.5, 2.0),
        "weight_middle": gaussian(splits[2], (LAYERS - 2, 9, CH, CH), (9 * CH) ** -0.5, 0.25),
        "weight_last": gaussian(splits[3], (9, CH), (9 * CH) ** -0.5, 0.25),
        "moveout_maps": gaussian(splits[4], (OB, NT, NT), NT ** -0.5, 0.25),
        "block_offset": with_ends(jax.random.randint(splits[5], (NBLOCKS,), 0, OB), jax.random.fold_in(splits[5], 1), 0, OB - 1).astype(jnp.int32),
        "block_target": different_ones(splits[6], NBLOCKS, MBLK, 1, 512),
    }


def convolve(signal, kernel):
    breadth = signal.shape[1] - 2
    length = signal.shape[3]
    padded = jnp.pad(signal.astype(jnp.float32), ((0, 0), (0, 0), (0, 0), (1, 1)))
    kernel_wide = kernel.astype(jnp.float32)
    summed = jnp.zeros((signal.shape[0], breadth, kernel.shape[1], length), jnp.float32)
    for across in range(3):
        for delay in range(3):
            window = padded[:, across:across + breadth, :, delay:delay + length]
            summed = summed + jnp.einsum("srct,oc->srot", window, kernel_wide[3 * across + delay], precision=lax.Precision.HIGHEST)
    return summed


def reference(shot_data, weight_first, weight_middle, weight_last, moveout_maps, block_offset, block_target):
    kernels = [weight_first.reshape(9, CH, 1)]
    for number in range(LAYERS - 2):
        kernels.append(weight_middle[number])
    kernels.append(weight_last.reshape(9, 1, CH))

    def denoise_shot(trace_set):
        signal = trace_set[None, :, None, :]
        summed = None
        for number in range(LAYERS):
            padded = jnp.pad(signal, ((0, 0), (1, 1), (0, 0), (0, 0)))
            summed = convolve(padded, kernels[number])
            if number < LAYERS - 1:
                signal = jnp.maximum(summed, 0.0).astype(jnp.bfloat16)
        return (trace_set.astype(jnp.float32) - summed[0, :, 0, :]).astype(jnp.bfloat16)

    denoised = lax.map(denoise_shot, shot_data)
    blocks = denoised.reshape(N_GRP, SH, N_TILE, RD, NT).transpose(0, 2, 1, 3, 4).reshape(NBLOCKS, BLK, NT)

    def correct_block(pair):
        block_rows, offset_bin = pair
        return jnp.dot(block_rows, moveout_maps[offset_bin], preferred_element_type=jnp.float32)

    corrected = lax.map(correct_block, (blocks, block_offset))
    stacked = jax.ops.segment_sum(corrected, block_target[:, 0], num_segments=MBLK)
    return denoised, stacked
```

```python
import jax
import jax.numpy as jnp
import numpy as np
from jax import lax
from jax.experimental import pallas as pl
from jax.experimental.pallas import tpu as pltpu
from jax.sharding import PartitionSpec as P

CH = 64
RD = 8
SH = 32
NT = 512
HALF = NT // 2
BLK = 128
PER_STEP = 2
SHOTS_PER_BLOCK = BLK // RD
F32 = jnp.float32
BF16 = jnp.bfloat16


def at_lane(shape, lane):
    return lax.broadcasted_iota(jnp.int32, shape, 1) % HALF == lane


def delayed(rows):
    return jnp.where(at_lane(rows.shape, 0), 0.0, pltpu.roll(rows, 1, 1))


def advanced(rows):
    return jnp.where(at_lane(rows.shape, HALF - 1), 0.0, pltpu.roll(rows, rows.shape[1] - 1, 1))


def denoise_body(
    offset_ref, low_ref, own_ref, high_ref, first_ref, middle_ref, last_ref, map_ref, *rest
):
    denoised_ref, corrected_ref, slots, h1, h2, cleaned = rest[-6:]
    step = pl.program_id(0)
    shots = own_ref.shape[0]

    @pl.when(step == 0)
    def split_samples():
        time = lax.broadcasted_iota(jnp.int32, (NT, 4 * HALF), 0)
        lane = lax.broadcasted_iota(jnp.int32, (NT, 4 * HALF), 1)
        split = (time == 2 * (lane % HALF) + lane // HALF - 1).astype(F32).astype(BF16)
        for side, ref in enumerate((low_ref, own_ref, high_ref)):
            taken = jnp.dot(ref[...].reshape(shots * RD, NT), split, preferred_element_type=F32)
            for slot in range(4):
                row = (4 * side + slot) * RD
                part = taken[:, slot * HALF : (slot + 1) * HALF]
                slots[:, row : row + RD, :] = part.reshape(shots, RD, HALF)

    for each in range(PER_STEP):
        lanes = slice(each * HALF, (each + 1) * HALF)
        taps = slots[step * PER_STEP + each].astype(BF16)
        summed = jnp.dot(first_ref[...], taps, preferred_element_type=F32)
        active = jnp.maximum(summed, 0.0)
        for receiver in range(RD + 4):
            pair = active[receiver * 2 * CH : (receiver + 1) * 2 * CH]
            row = receiver * 4 * CH
            h1[row + CH : row + 3 * CH, lanes] = pair.astype(BF16)
            h1[row : row + CH, lanes] = delayed(pair[CH:]).astype(BF16)
            h1[row + 3 * CH : row + 4 * CH, lanes] = advanced(pair[:CH]).astype(BF16)
    for receiver in range(RD + 2):
        window = h1[receiver * 4 * CH : (receiver + 3) * 4 * CH, :]
        summed = jnp.dot(middle_ref[...], window, preferred_element_type=F32)
        h2[receiver * 2 * CH : (receiver + 1) * 2 * CH, :] = jnp.maximum(summed, 0.0).astype(BF16)
    parts = jnp.dot(last_ref[...], h2[...], preferred_element_type=F32)
    even = parts[:RD] + delayed(parts[2 * RD : 3 * RD])
    odd = parts[RD : 2 * RD] + advanced(parts[3 * RD :])
    for each in range(PER_STEP):
        lanes = slice(each * HALF, (each + 1) * HALF)
        shot = step * PER_STEP + each
        rows = pl.ds(pl.multiple_of(shot * RD, RD), RD)
        cleaned[rows, :HALF] = slots[shot, 5 * RD : 6 * RD, :] - even[:, lanes]
        cleaned[rows, HALF:] = slots[shot, 6 * RD : 7 * RD, :] - odd[:, lanes]

    @pl.when(step == pl.num_programs(0) - 1)
    def merge_samples():
        lane = lax.broadcasted_iota(jnp.int32, (NT, NT), 0)
        time = lax.broadcasted_iota(jnp.int32, (NT, NT), 1)
        merge = (time == 2 * (lane % HALF) + lane // HALF).astype(F32).astype(BF16)
        traces = jnp.dot(cleaned[...].astype(BF16), merge, preferred_element_type=F32).astype(BF16)
        denoised_ref[...] = traces.reshape(shots, RD, NT)
        moved = jnp.dot(traces, map_ref[0], preferred_element_type=F32)
        corrected_ref[...] = moved.reshape(corrected_ref.shape)


def denoise_block(number, offsets, low, own, high, weights, moveout_maps, before):
    shots = SHOTS_PER_BLOCK
    part = pl.BlockSpec((shots, RD, NT), lambda i, o: (number, 0, 0))
    whole = [pl.BlockSpec(w.shape, lambda i, o: (0, 0)) for w in weights]
    chosen = pl.BlockSpec((1, NT, NT), lambda i, o: (o[number], 0, 0))
    held = [] if before is None else [before]
    owners = lax.axis_size("tile")
    return pl.pallas_call(
        denoise_body,
        out_shape=(
            jax.ShapeDtypeStruct((SH, RD, NT), BF16),
            jax.ShapeDtypeStruct((owners, BLK // owners, NT), F32),
        ),
        grid_spec=pltpu.PrefetchScalarGridSpec(
            num_scalar_prefetch=1,
            grid=(shots // PER_STEP,),
            in_specs=[part] * 3 + whole + [chosen] + [pl.BlockSpec(memory_space=pl.ANY)] * len(held),
            out_specs=(part, pl.BlockSpec((owners, BLK // owners, NT), lambda i, o: (0, 0, 0))),
            scratch_shapes=[
                pltpu.VMEM((shots, 12 * RD, HALF), F32),
                pltpu.VMEM(((RD + 4) * 4 * CH, PER_STEP * HALF), BF16),
                pltpu.VMEM(((RD + 2) * 2 * CH, PER_STEP * HALF), BF16),
                pltpu.VMEM((shots * RD, NT), F32),
            ],
        ),
        input_output_aliases={8: 0} if held else {},
        compiler_params=pltpu.CompilerParams(
            dimension_semantics=("arbitrary",), vmem_limit_bytes=48 << 20
        ),
        name="denoise",
    )(offsets, low, own, high, *weights, moveout_maps, *held)


def first_places():
    places = np.zeros((RD + 4, 2, 12 * RD, 9), np.float32)
    for receiver in range(RD + 4):
        for phase in range(2):
            for tap in range(9):
                across, delay = divmod(tap, 3)
                side, row = divmod(receiver - 2 + across - 1 + RD, RD)
                places[receiver, phase, (4 * side + phase + delay) * RD + row, tap] = 1
    return places


def place_weights(weight_first, weight_middle, weight_last):
    tile = lax.axis_index("tile")
    low = (tile > 0).astype(F32)
    high = (tile < lax.axis_size("tile") - 1).astype(F32)
    one = jnp.ones((), F32)
    inside = jnp.stack([low] * 2 + [one] * RD + [high] * 2)
    first = jnp.einsum(
        "rpkn,nc->rpck", jnp.asarray(first_places(), BF16), weight_first, preferred_element_type=F32
    )
    first = (first * inside[:, None, None, None]).astype(BF16).reshape((RD + 4) * 2 * CH, 12 * RD)
    taps = weight_middle.reshape(3, 3, CH, CH).transpose(2, 0, 1, 3)
    middle = jnp.stack(
        [jnp.pad(taps, ((0, 0), (0, 0), (phase, 1 - phase), (0, 0))) for phase in range(2)]
    ).reshape(2 * CH, 12 * CH)
    taps = weight_last.reshape(3, 3, CH)
    none = jnp.zeros((3, CH), BF16)
    kinds = jnp.stack(
        [
            jnp.stack([taps[:, 1], taps[:, 2]], 1),
            jnp.stack([taps[:, 0], taps[:, 1]], 1),
            jnp.stack([none, taps[:, 0]], 1),
            jnp.stack([taps[:, 2], none], 1),
        ]
    ).reshape(4, 6 * CH)
    last = jnp.stack(
        [jnp.pad(kinds, ((0, 0), (r * 2 * CH, (RD - 1 - r) * 2 * CH))) for r in range(RD)], 1
    )
    inside = jnp.repeat(inside[1:-1], 2 * CH, total_repeat_length=(RD + 2) * 2 * CH)
    last = (last.astype(F32) * inside).astype(BF16).reshape(4 * RD, (RD + 2) * 2 * CH)
    return first, middle, last


def stack_kernel(place_ref, early_ref, late_ref, total_ref):
    total_ref[...] = jnp.zeros_like(total_ref)
    for tile in range(early_ref.shape[0]):
        for number, ref in enumerate((early_ref, late_ref)):
            place = place_ref[tile, number]
            total_ref[place] = total_ref[place] + ref[tile]


def stack(places, early, late, count):
    return pl.pallas_call(
        stack_kernel,
        out_shape=jax.ShapeDtypeStruct((count, *early.shape[1:]), F32),
        in_specs=[
            pl.BlockSpec(memory_space=pltpu.SMEM),
            pl.BlockSpec(memory_space=pltpu.VMEM),
            pl.BlockSpec(memory_space=pltpu.VMEM),
        ],
        out_specs=pl.BlockSpec(memory_space=pltpu.VMEM),
        name="stack",
    )(places, early, late)


def on_device(
    shot_data, weight_first, weight_middle, weight_last, moveout_maps, block_offset, block_target
):
    tiles, groups = lax.axis_size("tile"), lax.axis_size("grp")
    low = lax.ppermute(shot_data, "tile", [(i, i + 1) for i in range(tiles - 1)])
    high = lax.ppermute(shot_data, "tile", [(i + 1, i) for i in range(tiles - 1)])
    weights = place_weights(weight_first, weight_middle, weight_last)
    targets = lax.all_gather(block_target[:, 0], "tile")
    count = 32
    owned = count // groups
    group = lax.axis_index("grp")
    places = ((targets // owned - group) % groups) * owned + targets % owned

    denoised, early = denoise_block(
        0, block_offset, low, shot_data, high, weights, moveout_maps, None
    )
    early = lax.all_to_all(early, "tile", 0, 0, tiled=True)
    denoised, late = denoise_block(
        1, block_offset, low, shot_data, high, weights, moveout_maps, denoised
    )
    late = lax.all_to_all(late, "tile", 0, 0, tiled=True)
    parts = stack(places, early, late, count).reshape(groups, owned, -1, NT)
    stacked = parts[0]
    for ahead in range(1, groups):
        route = [(g, (g + ahead) % groups) for g in range(groups)]
        stacked = stacked + lax.ppermute(parts[ahead], "grp", route)
    return denoised, stacked


def solution(mesh):
    in_specs = (
        P("grp", "tile", None),
        P(),
        P(),
        P(),
        P(),
        P(("grp", "tile")),
        P(("grp", "tile"), None),
    )
    out_specs = (P("grp", "tile", None), P("grp", "tile", None))
    return jax.shard_map(
        on_device, mesh=mesh, in_specs=in_specs, out_specs=out_specs, check_vma=False
    )
```

```python
import jax
import jax.numpy as jnp
import numpy as np
from jax import lax
from jax.experimental import pallas as pl
from jax.experimental.pallas import tpu as pltpu
from jax.sharding import PartitionSpec as P

CH = 64
RD = 8
SH = 32
NT = 512
HALF = NT // 2
BLK = 128
MBLK = 32
PER_STEP = 2
F32 = jnp.float32
BF16 = jnp.bfloat16


def at_lane(shape, lane):
    return lax.broadcasted_iota(jnp.int32, shape, 1) % HALF == lane


def delayed(rows):
    return jnp.where(at_lane(rows.shape, 0), 0.0, pltpu.roll(rows, 1, 1))


def advanced(rows):
    return jnp.where(at_lane(rows.shape, HALF - 1), 0.0, pltpu.roll(rows, rows.shape[1] - 1, 1))


def denoise_body(
    offset_ref, low_ref, own_ref, high_ref, first_ref, middle_ref, last_ref, *rest
):
    *map_refs, denoised_ref, corrected_ref, slots, h1, h2, cleaned = rest
    step = pl.program_id(0)
    shots = own_ref.shape[0]

    @pl.when(step == 0)
    def split_samples():
        time = lax.broadcasted_iota(jnp.int32, (NT, 4 * HALF), 0)
        lane = lax.broadcasted_iota(jnp.int32, (NT, 4 * HALF), 1)
        split = (time == 2 * (lane % HALF) + lane // HALF - 1).astype(F32).astype(BF16)
        for side, ref in enumerate((low_ref, own_ref, high_ref)):
            taken = jnp.dot(ref[...].reshape(shots * RD, NT), split, preferred_element_type=F32)
            for slot in range(4):
                row = (4 * side + slot) * RD
                part = taken[:, slot * HALF : (slot + 1) * HALF]
                slots[:, row : row + RD, :] = part.reshape(shots, RD, HALF)

    for each in range(PER_STEP):
        lanes = slice(each * HALF, (each + 1) * HALF)
        taps = slots[step * PER_STEP + each].astype(BF16)
        summed = jnp.dot(first_ref[...], taps, preferred_element_type=F32)
        active = jnp.maximum(summed, 0.0)
        for receiver in range(RD + 4):
            pair = active[receiver * 2 * CH : (receiver + 1) * 2 * CH]
            row = receiver * 4 * CH
            h1[row + CH : row + 3 * CH, lanes] = pair.astype(BF16)
            h1[row : row + CH, lanes] = delayed(pair[CH:]).astype(BF16)
            h1[row + 3 * CH : row + 4 * CH, lanes] = advanced(pair[:CH]).astype(BF16)
    for receiver in range(RD + 2):
        window = h1[receiver * 4 * CH : (receiver + 3) * 4 * CH, :]
        summed = jnp.dot(middle_ref[...], window, preferred_element_type=F32)
        h2[receiver * 2 * CH : (receiver + 1) * 2 * CH, :] = jnp.maximum(summed, 0.0).astype(BF16)
    parts = jnp.dot(last_ref[...], h2[...], preferred_element_type=F32)
    even = parts[:RD] + delayed(parts[2 * RD : 3 * RD])
    odd = parts[RD : 2 * RD] + advanced(parts[3 * RD :])
    for each in range(PER_STEP):
        lanes = slice(each * HALF, (each + 1) * HALF)
        shot = step * PER_STEP + each
        rows = pl.ds(pl.multiple_of(shot * RD, RD), RD)
        cleaned[rows, :HALF] = slots[shot, 5 * RD : 6 * RD, :] - even[:, lanes]
        cleaned[rows, HALF:] = slots[shot, 6 * RD : 7 * RD, :] - odd[:, lanes]

    @pl.when(step == pl.num_programs(0) - 1)
    def merge_samples():
        lane = lax.broadcasted_iota(jnp.int32, (NT, NT), 0)
        time = lax.broadcasted_iota(jnp.int32, (NT, NT), 1)
        merge = (time == 2 * (lane % HALF) + lane // HALF).astype(F32).astype(BF16)
        traces = jnp.dot(cleaned[...].astype(BF16), merge, preferred_element_type=F32).astype(BF16)
        denoised_ref[...] = traces.reshape(shots, RD, NT)
        owners = corrected_ref.shape[0]
        moved = []
        for number, ref in enumerate(map_refs):
            block = traces[number * BLK : (number + 1) * BLK]
            block = jnp.dot(block, ref[0], preferred_element_type=F32)
            moved.append(block.reshape(owners, BLK // owners, NT))
        corrected_ref[...] = jnp.concatenate(moved, axis=1)


def denoise(offsets, low, own, high, weights, moveout_maps):
    shots, blocks = own.shape[0], offsets.shape[0]
    part = pl.BlockSpec(own.shape, lambda i, o: (0, 0, 0))
    whole = [pl.BlockSpec(w.shape, lambda i, o: (0, 0)) for w in weights]
    chosen = [
        pl.BlockSpec((1, NT, NT), lambda i, o, number=number: (o[number], 0, 0))
        for number in range(blocks)
    ]
    owners = lax.axis_size("tile")
    sent = (owners, blocks * BLK // owners, NT)
    own = pltpu.with_memory_space_constraint(own, pltpu.HBM)
    maps = pltpu.with_memory_space_constraint(moveout_maps, pltpu.HBM)
    macs = shots * RD * NT * CH * (9 * CH + 18)
    return pl.pallas_call(
        denoise_body,
        out_shape=(jax.ShapeDtypeStruct(own.shape, BF16), jax.ShapeDtypeStruct(sent, F32)),
        grid_spec=pltpu.PrefetchScalarGridSpec(
            num_scalar_prefetch=1,
            grid=(shots // PER_STEP,),
            in_specs=[part] * 3 + whole + chosen,
            out_specs=(part, pl.BlockSpec(sent, lambda i, o: (0, 0, 0))),
            scratch_shapes=[
                pltpu.VMEM((shots, 12 * RD, HALF), F32),
                pltpu.VMEM(((RD + 4) * 4 * CH, PER_STEP * HALF), BF16),
                pltpu.VMEM(((RD + 2) * 2 * CH, PER_STEP * HALF), BF16),
                pltpu.VMEM((shots * RD, NT), F32),
            ],
        ),
        compiler_params=pltpu.CompilerParams(
            dimension_semantics=("arbitrary",), vmem_limit_bytes=48 << 20
        ),
        cost_estimate=pl.CostEstimate(flops=2 * macs, transcendentals=0, bytes_accessed=8 << 20),
        name="denoise",
    )(offsets, low, own, high, *weights, *[maps] * blocks)


def first_places():
    places = np.zeros((RD + 4, 2, 12 * RD, 9), np.float32)
    for receiver in range(RD + 4):
        for phase in range(2):
            for tap in range(9):
                across, delay = divmod(tap, 3)
                side, row = divmod(receiver - 2 + across - 1 + RD, RD)
                places[receiver, phase, (4 * side + phase + delay) * RD + row, tap] = 1
    return places


def place_weights(weight_first, weight_middle, weight_last):
    tile = lax.axis_index("tile")
    low = (tile > 0).astype(F32)
    high = (tile < lax.axis_size("tile") - 1).astype(F32)
    one = jnp.ones((), F32)
    inside = jnp.stack([low] * 2 + [one] * RD + [high] * 2)
    first = jnp.einsum(
        "rpkn,nc->rpck", jnp.asarray(first_places(), BF16), weight_first, preferred_element_type=F32
    )
    first = (first * inside[:, None, None, None]).astype(BF16).reshape((RD + 4) * 2 * CH, 12 * RD)
    taps = weight_middle.reshape(3, 3, CH, CH).transpose(2, 0, 1, 3)
    middle = jnp.stack(
        [jnp.pad(taps, ((0, 0), (0, 0), (phase, 1 - phase), (0, 0))) for phase in range(2)]
    ).reshape(2 * CH, 12 * CH)
    taps = weight_last.reshape(3, 3, CH)
    none = jnp.zeros((3, CH), BF16)
    kinds = jnp.stack(
        [
            jnp.stack([taps[:, 1], taps[:, 2]], 1),
            jnp.stack([taps[:, 0], taps[:, 1]], 1),
            jnp.stack([none, taps[:, 0]], 1),
            jnp.stack([taps[:, 2], none], 1),
        ]
    ).reshape(4, 6 * CH)
    last = jnp.stack(
        [jnp.pad(kinds, ((0, 0), (r * 2 * CH, (RD - 1 - r) * 2 * CH))) for r in range(RD)], 1
    )
    inside = jnp.repeat(inside[1:-1], 2 * CH, total_repeat_length=(RD + 2) * 2 * CH)
    last = (last.astype(F32) * inside).astype(BF16).reshape(4 * RD, (RD + 2) * 2 * CH)
    return first, middle, last


def stack_body(place_ref, corrected_ref, *refs):
    *part_refs, total = refs
    total[...] = jnp.zeros_like(total)
    rows = total.shape[1]
    for tile in range(corrected_ref.shape[0]):
        for number in range(corrected_ref.shape[1] // rows):
            place = place_ref[tile, number]
            held = corrected_ref[tile, number * rows : (number + 1) * rows, :]
            total[place] = total[place] + held
    for ahead, ref in enumerate(part_refs):
        ref[...] = total[ahead * ref.shape[0] : (ahead + 1) * ref.shape[0]]


def stack(places, corrected, groups, owned):
    rows = corrected.shape[1] // places.shape[1]
    part = jax.ShapeDtypeStruct((owned, rows, NT), F32)
    return pl.pallas_call(
        stack_body,
        out_shape=(part,) * groups,
        in_specs=[
            pl.BlockSpec(memory_space=pltpu.SMEM),
            pl.BlockSpec(memory_space=pltpu.VMEM),
        ],
        out_specs=(pl.BlockSpec(memory_space=pltpu.VMEM),) * groups,
        scratch_shapes=[pltpu.VMEM((groups * owned, rows, NT), F32)],
        name="stack",
    )(places, corrected)


def on_device(
    shot_data, weight_first, weight_middle, weight_last, moveout_maps, block_offset, block_target
):
    tiles, groups = lax.axis_size("tile"), lax.axis_size("grp")
    low = lax.ppermute(shot_data, "tile", [(i, i + 1) for i in range(tiles - 1)])
    high = lax.ppermute(shot_data, "tile", [(i + 1, i) for i in range(tiles - 1)])
    weights = place_weights(weight_first, weight_middle, weight_last)
    padded = jnp.pad(block_target.reshape(1, 1, -1), ((0, 0), (0, 0), (0, 126)))
    targets = lax.all_gather(padded, "tile", tiled=True)[:, 0, :2]
    owned = MBLK // groups
    ahead = (targets // owned - lax.axis_index("grp")) % groups
    places = ahead * owned + targets % owned

    denoised, corrected = denoise(block_offset, low, shot_data, high, weights, moveout_maps)
    corrected = lax.all_to_all(corrected, "tile", 0, 0, tiled=True)
    stacked, *parts = stack(places, corrected, groups, owned)
    for ahead, part in enumerate(parts, 1):
        route = [(g, (g + ahead) % groups) for g in range(groups)]
        stacked = stacked + lax.ppermute(part, "grp", route)
    return denoised, stacked


def solution(mesh):
    in_specs = (
        P("grp", "tile", None),
        P(),
        P(),
        P(),
        P(),
        P(("grp", "tile")),
        P(("grp", "tile"), None),
    )
    out_specs = (P("grp", "tile", None), P("grp", "tile", None))
    return jax.shard_map(
        on_device, mesh=mesh, in_specs=in_specs, out_specs=out_specs, check_vma=False
    )
```

```python
import jax
import jax.numpy as jnp
from jax import lax
from jax.experimental import pallas as pl
from jax.experimental.pallas import tpu as pltpu
from jax.sharding import PartitionSpec as P

CH = 64
RD = 8
SH = 32
NT = 512
OB = 8
BLK = 128
MBLK = 32
LANES = 128
UNIT = 256
UNITS = 2
HALF = NT // 2
OUTER = RD + 4
INNER = RD + 2
F32 = jnp.float32
BF16 = jnp.bfloat16


def at_lane(shape, lane):
    return lax.broadcasted_iota(jnp.int32, shape, 1) % HALF == lane


def delayed(rows):
    return jnp.where(at_lane(rows.shape, 0), jnp.zeros_like(rows), pltpu.roll(rows, 1, 1))


def advanced(rows):
    last = rows.shape[1] - 1
    return jnp.where(at_lane(rows.shape, HALF - 1), jnp.zeros_like(rows), pltpu.roll(rows, last, 1))


def one_hot(condition):
    return condition.astype(F32).astype(BF16)


def prepare_body(tap1_ref, tap2_ref, tap3_ref, own_ref, first_ref, middle_ref, last_ref, split_ref, slots_ref, wide):
    tile = lax.axis_index("tile")
    low = (tile > 0).astype(F32)
    high = (tile < lax.axis_size("tile") - 1).astype(F32)

    shape = (9, UNIT)
    tap = lax.broadcasted_iota(jnp.int32, shape, 0)
    column = lax.broadcasted_iota(jnp.int32, shape, 1)
    across = column // 32 * RD + column % RD - RD + 3
    delay = column // RD % 4
    for receiver in range(OUTER):
        inside = low if receiver < 2 else high if receiver >= OUTER - 2 else None
        for phase in range(2):
            a, d = across - receiver, delay - phase
            place = (tap == 3 * a + d) & (a >= 0) & (a <= 2) & (d >= 0) & (d <= 2) & (column < 96)
            place = place.astype(F32)
            if inside is not None:
                place = place * inside
            block = lax.dot_general(
                tap1_ref[...], place.astype(BF16), (((0,), (0,)), ((), ())), preferred_element_type=F32
            )
            row = (2 * receiver + phase) * CH
            first_ref[row : row + CH, :] = block.astype(BF16)

    none = jnp.zeros((CH, CH), BF16)
    for across in range(3):
        taps = [tap2_ref[(3 * across + d) * CH : (3 * across + d + 1) * CH, :] for d in range(3)]
        lanes = slice(across * UNIT, (across + 1) * UNIT)
        middle_ref[:CH, lanes] = jnp.concatenate([*taps, none], axis=1)
        middle_ref[CH:, lanes] = jnp.concatenate([none, *taps], axis=1)

    none = jnp.zeros((1, CH), F32)
    taps = [tap3_ref[k : k + 1, :].astype(F32) for k in range(9)]
    kinds = [
        [taps[3 * a + 1] for a in range(3)], [taps[3 * a + 2] for a in range(3)],
        [taps[3 * a] for a in range(3)], [taps[3 * a + 1] for a in range(3)],
        [none] * 3, [taps[3 * a] for a in range(3)],
        [taps[3 * a + 2] for a in range(3)], [none] * 3,
    ]
    wide[...] = jnp.zeros_like(wide)
    for kind in range(4):
        row = [t for pair in zip(kinds[2 * kind], kinds[2 * kind + 1]) for t in pair]
        row = jnp.concatenate(row, axis=1)
        for receiver in range(RD):
            at = kind * RD + receiver
            wide[at : at + 1, receiver * 2 * CH : (receiver + 3) * 2 * CH] = row
    wide[:, : 2 * CH] = wide[:, : 2 * CH] * low
    wide[:, (INNER - 1) * 2 * CH :] = wide[:, (INNER - 1) * 2 * CH :] * high
    last_ref[...] = wide[...].astype(BF16)

    time = lax.broadcasted_iota(jnp.int32, (NT, 4 * HALF), 0)
    lane = lax.broadcasted_iota(jnp.int32, (NT, 4 * HALF), 1)
    split = one_hot(time == 2 * (lane % HALF) + lane // HALF - 1)
    split_ref[...] = split
    shots = own_ref.shape[0]
    taken = jnp.dot(own_ref[...].reshape(shots * RD, NT), split, preferred_element_type=F32)
    parts = [taken[:, s * HALF : (s + 1) * HALF].reshape(shots, RD, HALF) for s in range(4)]
    slots_ref[...] = jnp.concatenate(parts, axis=1).astype(BF16)


def prepare(weight_first, weight_middle, weight_last, own):
    shapes = (
        (OUTER * 2 * CH, UNIT),
        (2 * CH, 3 * UNIT),
        (4 * RD, INNER * 2 * CH),
        (NT, 4 * HALF),
        (own.shape[0], 4 * RD, HALF),
    )
    return pl.pallas_call(
        prepare_body,
        out_shape=tuple(jax.ShapeDtypeStruct(s, BF16) for s in shapes),
        scratch_shapes=[pltpu.VMEM(shapes[2], F32)],
        compiler_params=pltpu.CompilerParams(vmem_limit_bytes=24 << 20),
        name="prepare",
    )(weight_first, weight_middle.reshape(9 * CH, CH), weight_last, own)


def product(accs, lhs, rhs, use):
    rows, depth = lhs.shape
    for n in range(rhs.shape[1] // UNIT):
        held = accs[n % UNITS]
        for k in range(depth // UNIT):
            piece = rhs[k * UNIT : (k + 1) * UNIT, n * UNIT : (n + 1) * UNIT]
            pltpu.matmul_push_rhs(piece, k % 2, n % UNITS)
            for c in range(rows // BLK):
                piece = lhs[c * BLK : (c + 1) * BLK, k * UNIT : (k + 1) * UNIT]
                pltpu.matmul_acc_lhs(held[c], piece, load_staged_rhs=k % 2 if c == 0 else None)
        for c in range(rows // BLK):
            use(n, c, pltpu.matmul_pop(held[c]))


def run(jobs):
    def push(number):
        for unit in range(UNITS):
            pltpu.matmul_push_rhs(jobs[number][0](unit), number % 2, unit)

    push(0)
    for number, (_, products, after) in enumerate(jobs):
        if number + 1 < len(jobs):
            push(number + 1)
        for n, (acc, lhs) in enumerate(products):
            for unit in range(UNITS):
                staged = number % 2 if n == 0 else None
                pltpu.matmul_acc_lhs(acc(unit), lhs(), load_staged_rhs=staged)
        for act in after:
            act()


def denoise_loop(
    offset_ref, target_ref, low_ref, high_ref, own, first_ref, middle_ref, last_ref, split_ref,
    denoised_ref, sent_ref, low, high, h1_even, h1_odd, h2_even, h2_odd, cleaned, rows4, accs,
):
    shots = own.shape[0]
    pairs = shots // UNITS
    per_block = BLK // RD

    for ref, held in ((low_ref, low), (high_ref, high)):
        def put(slot, c, part, held=held):
            part = part.astype(BF16).reshape(per_block, RD, HALF)
            held[c * per_block : (c + 1) * per_block, slot * RD : (slot + 1) * RD, :] = part

        product(accs, ref[...].reshape(shots * RD, NT), split_ref, put)

    def taps(pair):
        def right(unit):
            shot = pair * UNITS + unit
            rest = jnp.zeros((UNIT - 12 * RD, HALF), BF16)
            return jnp.concatenate([low[shot], own[shot], high[shot], rest], axis=0)

        return right

    def first_done(h1, receiver):
        def act():
            for unit in range(UNITS):
                both = jnp.maximum(pltpu.matmul_pop(accs[unit][receiver % 3]), 0.0).astype(BF16)
                h1[unit, receiver, CH : 3 * CH, :] = both
                h1[unit, receiver, :CH, :] = delayed(both[CH:])
                h1[unit, receiver, 3 * CH :, :] = advanced(both[:CH])

        return act

    def middle_done(h2, receiver):
        def act():
            for unit in range(UNITS):
                both = jnp.maximum(pltpu.matmul_pop(accs[unit][3 + receiver % 4]), 0.0)
                h2[unit, receiver * 2 * CH : (receiver + 1) * 2 * CH, :] = both.astype(BF16)

        return act

    def last_done(pair):
        def act():
            for unit in range(UNITS):
                shot = pair * UNITS + unit
                parts = pltpu.matmul_pop(accs[unit][7])
                seen = own[shot].astype(F32)
                rows = pl.ds(pl.multiple_of(shot * RD, RD), RD)
                even = parts[:RD] + delayed(parts[2 * RD : 3 * RD])
                odd = parts[RD : 2 * RD] + advanced(parts[3 * RD :])
                cleaned[rows, :HALF] = seen[RD : 2 * RD] - even
                cleaned[rows, HALF:] = seen[2 * RD : 3 * RD] - odd

        return act

    def first_job(pair, receivers):
        products = [
            (
                lambda unit, r=r: accs[unit][r % 3],
                lambda r=r: first_ref[r * 2 * CH : (r + 1) * 2 * CH, :],
            )
            for r in receivers
        ]
        return taps(pair), products, []

    def middle_job(h1, receiver):
        products = [
            (
                lambda unit, r=receiver - across: accs[unit][3 + r % 4],
                lambda across=across: middle_ref[:, across * UNIT : (across + 1) * UNIT],
            )
            for across in (2, 1, 0)
            if 0 <= receiver - across < INNER
        ]
        return lambda unit: h1[unit, receiver], products, []

    def last_job(h2, number):
        lanes = slice(number * UNIT, (number + 1) * UNIT)
        products = [(lambda unit: accs[unit][7], lambda: last_ref[:, lanes])]
        return lambda unit: h2[unit, lanes, :], products, []

    def stage(now, later, before):
        jobs = []
        for r in range(OUTER):
            if later and r % 3 == 0:
                jobs.append(first_job(later[0], range(r, r + 3)))
            if now:
                jobs.append(middle_job(now[0], r))
            if later:
                jobs[-1][2].append(first_done(later[1], r))
            if now and r >= 3:
                jobs[-1][2].append(middle_done(now[1], r - 3))
            if before and r % 2 == 1 and r < INNER:
                jobs.append(last_job(before[1], r // 2))
            if before and r == INNER:
                jobs[-1][2].append(last_done(before[0]))
        return jobs, [middle_done(now[1], INNER - 1)] if now else []

    def chain(*stages):
        jobs, tail = [], []
        for more, end in stages:
            more[0][2].extend(tail)
            jobs, tail = jobs + more, end
        jobs[-1][2].extend(tail)
        run(jobs)

    chain(stage(None, (0, h1_even), None))
    chain(stage((h1_even, h2_even), (1, h1_odd), None))

    def two(step, carry):
        pair = 2 * step + 1
        chain(
            stage((h1_odd, h2_odd), (pair + 1, h1_even), (pair - 1, h2_even)),
            stage((h1_even, h2_even), (pair + 2, h1_odd), (pair, h2_odd)),
        )
        return carry

    lax.fori_loop(0, (pairs - 2) // 2, two, 0)
    chain(stage((h1_odd, h2_odd), None, (pairs - 2, h2_even)))
    chain(([last_job(h2_odd, n) for n in range(INNER // 2)], [last_done(pairs - 1)]))

    lane = lax.broadcasted_iota(jnp.int32, (NT, NT), 0)
    time = lax.broadcasted_iota(jnp.int32, (NT, NT), 1)
    merge = one_hot(time == 2 * (lane % HALF) + lane // HALF)
    owners = sent_ref.shape[0]
    kept = BLK // owners

    def put(n, c, part):
        lanes = slice(n * UNIT, (n + 1) * UNIT)
        shot = slice(c * per_block, (c + 1) * per_block)
        denoised_ref[shot, :, lanes] = part.astype(BF16).reshape(per_block, RD, UNIT)
        rows4[:, c * kept : (c + 1) * kept, lanes] = part.reshape(owners, kept, UNIT)

    product(accs, cleaned[...].astype(BF16), merge, put)
    shape = (owners, kept, LANES // 2)
    for c in range(shots * RD // BLK):
        rows4[:, c * kept : (c + 1) * kept, NT : NT + LANES // 2] = jnp.full(shape, target_ref[c].astype(F32))
        rows4[:, c * kept : (c + 1) * kept, NT + LANES // 2 :] = jnp.full(shape, offset_ref[c].astype(F32))
    sent_ref[...] = rows4[...].astype(BF16)


def denoise_body(*refs):
    pl.run_scoped(
        lambda *accs: denoise_loop(*refs, (accs[:8], accs[8:])),
        *[
            pltpu.ACC(unit)((BLK if number < 7 else 4 * RD, UNIT), F32)
            for unit in range(UNITS)
            for number in range(8)
        ],
    )


def denoise(offsets, targets, low, high, slots, first, middle, last, split):
    shots, blocks = low.shape[0], offsets.shape[0]
    owners = lax.axis_size("tile")
    sent = (owners, blocks * BLK // owners, NT + LANES)
    scalars = pl.BlockSpec(memory_space=pltpu.SMEM)
    whole = pl.BlockSpec(memory_space=pltpu.VMEM)
    macs = shots * RD * NT * CH * (9 * CH + 18)
    return pl.pallas_call(
        denoise_body,
        out_shape=(jax.ShapeDtypeStruct((shots, RD, NT), BF16), jax.ShapeDtypeStruct(sent, BF16)),
        in_specs=[scalars] * 2 + [whole] * 7,
        out_specs=(whole, whole),
        scratch_shapes=[pltpu.VMEM((shots, 4 * RD, HALF), BF16)] * 2
        + [pltpu.VMEM((UNITS, OUTER, UNIT, HALF), BF16)] * 2
        + [pltpu.VMEM((UNITS, INNER * 2 * CH, HALF), BF16)] * 2
        + [pltpu.VMEM((shots * RD, NT), F32), pltpu.VMEM(sent, F32)],
        compiler_params=pltpu.CompilerParams(vmem_limit_bytes=40 << 20),
        cost_estimate=pl.CostEstimate(flops=2 * macs, transcendentals=0, bytes_accessed=4 << 20),
        name="denoise",
    )(offsets, targets, low, high, slots, first, middle, last, split)


def stack_body(came_ref, map_ref, *part_refs):
    tiles, kept, _ = came_ref.shape
    rows = kept * BLK // (SH * RD)
    count = tiles * kept
    came = came_ref[...].reshape(count, NT + LANES)
    target = came[:, NT : NT + 1].astype(F32).astype(jnp.int32)
    offset = came[:, NT + LANES // 2 : NT + LANES // 2 + 1].astype(F32)
    traces = came[:, :NT]
    none = jnp.zeros_like(traces)
    wide = [jnp.where(offset == o, traces, none) for o in range(OB)]
    corrected = jnp.dot(
        jnp.concatenate(wide, axis=1), map_ref[...], preferred_element_type=F32
    )
    groups = len(part_refs)
    owned = MBLK // groups
    ahead = (target // owned - lax.axis_index("grp") + groups) % groups
    place = ahead * owned + target % owned
    row = lax.broadcasted_iota(jnp.int32, (count, MBLK * rows), 0) % rows
    column = lax.broadcasted_iota(jnp.int32, (count, MBLK * rows), 1)
    chosen = one_hot((place == column // rows) & (row == column % rows))
    total = None
    for _ in range(3):
        part = corrected.astype(BF16)
        corrected = corrected - part.astype(F32)
        term = lax.dot_general(chosen, part, (((0,), (0,)), ((), ())), preferred_element_type=F32)
        total = term if total is None else total + term
    for number, ref in enumerate(part_refs):
        part = total[number * owned * rows : (number + 1) * owned * rows]
        ref[...] = part.reshape(ref.shape)


def stack(came, moveout_maps, groups):
    rows = came.shape[1] * BLK // (SH * RD)
    part = jax.ShapeDtypeStruct((MBLK // groups, rows, NT), F32)
    return pl.pallas_call(
        stack_body,
        out_shape=(part,) * groups,
        compiler_params=pltpu.CompilerParams(vmem_limit_bytes=40 << 20),
        name="stack",
    )(came, moveout_maps.reshape(OB * NT, NT))


def on_device(
    shot_data, weight_first, weight_middle, weight_last, moveout_maps, block_offset, block_target
):
    tiles, groups = lax.axis_size("tile"), lax.axis_size("grp")
    low = lax.ppermute(shot_data, "tile", [(i, i + 1) for i in range(tiles - 1)])
    high = lax.ppermute(shot_data, "tile", [(i + 1, i) for i in range(tiles - 1)])
    *weights, split, slots = prepare(weight_first, weight_middle, weight_last, shot_data)
    denoised, sent = denoise(
        block_offset, block_target.reshape(-1), low, high, slots, *weights, split
    )
    came = lax.all_to_all(sent, "tile", 0, 0, tiled=True)
    stacked, *parts = stack(came, moveout_maps, groups)
    for ahead, part in enumerate(parts, 1):
        route = [(g, (g + ahead) % groups) for g in range(groups)]
        stacked = stacked + lax.ppermute(part, "grp", route)
    return denoised, stacked


def solution(mesh):
    in_specs = (
        P("grp", "tile", None),
        P(),
        P(),
        P(),
        P(),
        P(("grp", "tile")),
        P(("grp", "tile"), None),
    )
    out_specs = (P("grp", "tile", None), P("grp", "tile", None))
    return jax.shard_map(
        on_device, mesh=mesh, in_specs=in_specs, out_specs=out_specs, check_vma=False
    )
```

```python
import jax
import jax.numpy as jnp
from jax import lax
from jax.experimental import pallas as pl
from jax.experimental.pallas import tpu as pltpu
from jax.sharding import PartitionSpec as P

CH = 64
RD = 8
SH = 32
NT = 512
OB = 8
BLK = 128
MBLK = 32
LANES = 128
UNIT = 256
UNITS = 2
HALF = NT // 2
OUTER = RD + 4
INNER = RD + 2
F32 = jnp.float32
BF16 = jnp.bfloat16


def at_lane(shape, lane):
    return lax.broadcasted_iota(jnp.int32, shape, 1) % HALF == lane


def delayed(rows):
    return jnp.where(at_lane(rows.shape, 0), jnp.zeros_like(rows), pltpu.roll(rows, 1, 1))


def advanced(rows):
    last = rows.shape[1] - 1
    return jnp.where(at_lane(rows.shape, HALF - 1), jnp.zeros_like(rows), pltpu.roll(rows, last, 1))


def one_hot(condition):
    return condition.astype(F32).astype(BF16)


def prepare_body(tap1_ref, tap2_ref, tap3_ref, own_ref, first_ref, middle_ref, last_ref, split_ref, slots_ref, wide):
    tile = lax.axis_index("tile")
    low = (tile > 0).astype(F32)
    high = (tile < lax.axis_size("tile") - 1).astype(F32)

    shape = (9, UNIT)
    tap = lax.broadcasted_iota(jnp.int32, shape, 0)
    column = lax.broadcasted_iota(jnp.int32, shape, 1)
    across = column // 32 * RD + column % RD - RD + 3
    delay = column // RD % 4
    for receiver in range(OUTER):
        inside = low if receiver < 2 else high if receiver >= OUTER - 2 else None
        for phase in range(2):
            a, d = across - receiver, delay - phase
            place = (tap == 3 * a + d) & (a >= 0) & (a <= 2) & (d >= 0) & (d <= 2) & (column < 96)
            place = place.astype(F32)
            if inside is not None:
                place = place * inside
            block = lax.dot_general(
                tap1_ref[...], place.astype(BF16), (((0,), (0,)), ((), ())), preferred_element_type=F32
            )
            row = (2 * receiver + phase) * CH
            first_ref[row : row + CH, :] = block.astype(BF16)

    none = jnp.zeros((CH, CH), BF16)
    for across in range(3):
        taps = [tap2_ref[(3 * across + d) * CH : (3 * across + d + 1) * CH, :] for d in range(3)]
        lanes = slice(across * UNIT, (across + 1) * UNIT)
        middle_ref[:CH, lanes] = jnp.concatenate([*taps, none], axis=1)
        middle_ref[CH:, lanes] = jnp.concatenate([none, *taps], axis=1)

    none = jnp.zeros((1, CH), F32)
    taps = [tap3_ref[k : k + 1, :].astype(F32) for k in range(9)]
    kinds = [
        [taps[3 * a + 1] for a in range(3)], [taps[3 * a + 2] for a in range(3)],
        [taps[3 * a] for a in range(3)], [taps[3 * a + 1] for a in range(3)],
        [none] * 3, [taps[3 * a] for a in range(3)],
        [taps[3 * a + 2] for a in range(3)], [none] * 3,
    ]
    wide[...] = jnp.zeros_like(wide)
    for kind in range(4):
        row = [t for pair in zip(kinds[2 * kind], kinds[2 * kind + 1]) for t in pair]
        row = jnp.concatenate(row, axis=1)
        for receiver in range(RD):
            at = kind * RD + receiver
            wide[at : at + 1, receiver * 2 * CH : (receiver + 3) * 2 * CH] = row
    wide[:, : 2 * CH] = wide[:, : 2 * CH] * low
    wide[:, (INNER - 1) * 2 * CH :] = wide[:, (INNER - 1) * 2 * CH :] * high
    last_ref[...] = wide[...].astype(BF16)

    time = lax.broadcasted_iota(jnp.int32, (NT, 4 * HALF), 0)
    lane = lax.broadcasted_iota(jnp.int32, (NT, 4 * HALF), 1)
    split = one_hot(time == 2 * (lane % HALF) + lane // HALF - 1)
    split_ref[...] = split
    shots = own_ref.shape[0]
    taken = jnp.dot(own_ref[...].reshape(shots * RD, NT), split, preferred_element_type=F32)
    parts = [taken[:, s * HALF : (s + 1) * HALF].reshape(shots, RD, HALF) for s in range(4)]
    slots_ref[...] = jnp.concatenate(parts, axis=1).astype(BF16)


def prepare(weight_first, weight_middle, weight_last, own):
    shapes = (
        (OUTER * 2 * CH, UNIT),
        (2 * CH, 3 * UNIT),
        (4 * RD, INNER * 2 * CH),
        (NT, 4 * HALF),
        (own.shape[0], 4 * RD, HALF),
    )
    return pl.pallas_call(
        prepare_body,
        out_shape=tuple(jax.ShapeDtypeStruct(s, BF16) for s in shapes),
        scratch_shapes=[pltpu.VMEM(shapes[2], F32)],
        compiler_params=pltpu.CompilerParams(vmem_limit_bytes=24 << 20),
        name="prepare",
    )(weight_first, weight_middle, weight_last, own)


def product(accs, lhs, rhs, use):
    rows, depth = lhs.shape
    for n in range(rhs.shape[1] // UNIT):
        held = accs[n % UNITS]
        for k in range(depth // UNIT):
            piece = rhs[k * UNIT : (k + 1) * UNIT, n * UNIT : (n + 1) * UNIT]
            pltpu.matmul_push_rhs(piece, k % 2, n % UNITS)
            for c in range(rows // BLK):
                piece = lhs[c * BLK : (c + 1) * BLK, k * UNIT : (k + 1) * UNIT]
                pltpu.matmul_acc_lhs(held[c], piece, load_staged_rhs=k % 2 if c == 0 else None)
        for c in range(rows // BLK):
            use(n, c, pltpu.matmul_pop(held[c]))


def run(jobs):
    def push(number):
        for unit in range(UNITS):
            pltpu.matmul_push_rhs(jobs[number][0](unit), number % 2, unit)

    push(0)
    for number, (_, products, after) in enumerate(jobs):
        if number + 1 < len(jobs):
            push(number + 1)
        for n, (acc, lhs) in enumerate(products):
            for unit in range(UNITS):
                staged = number % 2 if n == 0 else None
                pltpu.matmul_acc_lhs(acc(unit), lhs(), load_staged_rhs=staged)
        for act in after:
            act()


def denoise_loop(
    offset_ref, target_ref, low_ref, high_ref, own, first_ref, middle_ref, last_ref, split_ref,
    denoised_ref, sent_ref, low, high, h1_even, h1_odd, h2_even, h2_odd, cleaned, rows4, accs,
):
    shots = own.shape[0]
    pairs = shots // UNITS
    per_block = BLK // RD

    for ref, held in ((low_ref, low), (high_ref, high)):
        def put(slot, c, part, held=held):
            part = part.astype(BF16).reshape(per_block, RD, HALF)
            held[c * per_block : (c + 1) * per_block, slot * RD : (slot + 1) * RD, :] = part

        product(accs, ref[...].reshape(shots * RD, NT), split_ref, put)

    def taps(pair):
        def right(unit):
            shot = pair * UNITS + unit
            rest = jnp.zeros((UNIT - 12 * RD, HALF), BF16)
            return jnp.concatenate([low[shot], own[shot], high[shot], rest], axis=0)

        return right

    def first_done(h1, receiver):
        def act():
            for unit in range(UNITS):
                both = jnp.maximum(pltpu.matmul_pop(accs[unit][receiver % 3]), 0.0).astype(BF16)
                h1[unit, receiver, CH : 3 * CH, :] = both
                h1[unit, receiver, :CH, :] = delayed(both[CH:])
                h1[unit, receiver, 3 * CH :, :] = advanced(both[:CH])

        return act

    def middle_done(h2, receiver):
        def act():
            for unit in range(UNITS):
                both = jnp.maximum(pltpu.matmul_pop(accs[unit][3 + receiver % 4]), 0.0)
                h2[unit, receiver * 2 * CH : (receiver + 1) * 2 * CH, :] = both.astype(BF16)

        return act

    def last_done(pair):
        def act():
            for unit in range(UNITS):
                shot = pair * UNITS + unit
                parts = pltpu.matmul_pop(accs[unit][7])
                seen = own[shot].astype(F32)
                rows = pl.ds(pl.multiple_of(shot * RD, RD), RD)
                even = parts[:RD] + delayed(parts[2 * RD : 3 * RD])
                odd = parts[RD : 2 * RD] + advanced(parts[3 * RD :])
                cleaned[rows, :HALF] = seen[RD : 2 * RD] - even
                cleaned[rows, HALF:] = seen[2 * RD : 3 * RD] - odd

        return act

    def first_job(pair, receivers):
        products = [
            (
                lambda unit, r=r: accs[unit][r % 3],
                lambda r=r: first_ref[r * 2 * CH : (r + 1) * 2 * CH, :],
            )
            for r in receivers
        ]
        return taps(pair), products, []

    def middle_job(h1, receiver):
        products = [
            (
                lambda unit, r=receiver - across: accs[unit][3 + r % 4],
                lambda across=across: middle_ref[:, across * UNIT : (across + 1) * UNIT],
            )
            for across in (2, 1, 0)
            if 0 <= receiver - across < INNER
        ]
        return lambda unit: h1[unit, receiver], products, []

    def last_job(h2, number):
        lanes = slice(number * UNIT, (number + 1) * UNIT)
        products = [(lambda unit: accs[unit][7], lambda: last_ref[:, lanes])]
        return lambda unit: h2[unit, lanes, :], products, []

    def stage(now, later, before):
        jobs = []
        for r in range(OUTER):
            if later and r % 3 == 0:
                jobs.append(first_job(later[0], range(r, r + 3)))
            if now:
                jobs.append(middle_job(now[0], r))
            if later:
                jobs[-1][2].append(first_done(later[1], r))
            if now and r >= 3:
                jobs[-1][2].append(middle_done(now[1], r - 3))
            if before and r % 2 == 1 and r < INNER:
                jobs.append(last_job(before[1], r // 2))
            if before and r == INNER:
                jobs[-1][2].append(last_done(before[0]))
        return jobs, [middle_done(now[1], INNER - 1)] if now else []

    def chain(*stages):
        jobs, tail = [], []
        for more, end in stages:
            more[0][2].extend(tail)
            jobs, tail = jobs + more, end
        jobs[-1][2].extend(tail)
        run(jobs)

    chain(stage(None, (0, h1_even), None))
    chain(stage((h1_even, h2_even), (1, h1_odd), None))

    def two(step, carry):
        pair = 2 * step + 1
        chain(
            stage((h1_odd, h2_odd), (pair + 1, h1_even), (pair - 1, h2_even)),
            stage((h1_even, h2_even), (pair + 2, h1_odd), (pair, h2_odd)),
        )
        return carry

    lax.fori_loop(0, (pairs - 2) // 2, two, 0)
    chain(stage((h1_odd, h2_odd), None, (pairs - 2, h2_even)))
    chain(([last_job(h2_odd, n) for n in range(INNER // 2)], [last_done(pairs - 1)]))

    lane = lax.broadcasted_iota(jnp.int32, (NT, NT), 0)
    time = lax.broadcasted_iota(jnp.int32, (NT, NT), 1)
    merge = one_hot(time == 2 * (lane % HALF) + lane // HALF)
    owners = sent_ref.shape[0]
    kept = BLK // owners

    def put(n, c, part):
        lanes = slice(n * UNIT, (n + 1) * UNIT)
        shot = slice(c * per_block, (c + 1) * per_block)
        denoised_ref[shot, :, lanes] = part.astype(BF16).reshape(per_block, RD, UNIT)
        rows4[:, c * kept : (c + 1) * kept, lanes] = part.reshape(owners, kept, UNIT)

    product(accs, cleaned[...].astype(BF16), merge, put)
    shape = (owners, kept, LANES // 2)
    for c in range(shots * RD // BLK):
        rows4[:, c * kept : (c + 1) * kept, NT : NT + LANES // 2] = jnp.full(shape, target_ref[c].astype(F32))
        rows4[:, c * kept : (c + 1) * kept, NT + LANES // 2 :] = jnp.full(shape, offset_ref[c].astype(F32))
    sent_ref[...] = rows4[...].astype(BF16)


def denoise_body(*refs):
    pl.run_scoped(
        lambda *accs: denoise_loop(*refs, (accs[:8], accs[8:])),
        *[
            pltpu.ACC(unit)((BLK if number < 7 else 4 * RD, UNIT), F32)
            for unit in range(UNITS)
            for number in range(8)
        ],
    )


def denoise(offsets, targets, low, high, slots, first, middle, last, split):
    shots, blocks = low.shape[0], offsets.shape[0]
    owners = lax.axis_size("tile")
    sent = (owners, blocks * BLK // owners, NT + LANES)
    scalars = pl.BlockSpec(memory_space=pltpu.SMEM)
    whole = pl.BlockSpec(memory_space=pltpu.VMEM)
    macs = shots * RD * NT * CH * (9 * CH + 18)
    return pl.pallas_call(
        denoise_body,
        out_shape=(jax.ShapeDtypeStruct((shots, RD, NT), BF16), jax.ShapeDtypeStruct(sent, BF16)),
        in_specs=[scalars] * 2 + [whole] * 7,
        out_specs=(whole, whole),
        scratch_shapes=[pltpu.VMEM((shots, 4 * RD, HALF), BF16)] * 2
        + [pltpu.VMEM((UNITS, OUTER, UNIT, HALF), BF16)] * 2
        + [pltpu.VMEM((UNITS, INNER * 2 * CH, HALF), BF16)] * 2
        + [pltpu.VMEM((shots * RD, NT), F32), pltpu.VMEM(sent, F32)],
        compiler_params=pltpu.CompilerParams(vmem_limit_bytes=40 << 20),
        cost_estimate=pl.CostEstimate(flops=2 * macs, transcendentals=0, bytes_accessed=4 << 20),
        name="denoise",
    )(offsets, targets, low, high, slots, first, middle, last, split)


def stack_body(came_ref, map_ref, *part_refs):
    tiles, kept, _ = came_ref.shape
    rows = kept * BLK // (SH * RD)
    count = tiles * kept
    came = came_ref[...].reshape(count, NT + LANES)
    target = came[:, NT : NT + 1].astype(F32).astype(jnp.int32)
    offset = came[:, NT + LANES // 2 : NT + LANES // 2 + 1].astype(F32)
    traces = came[:, :NT]
    none = jnp.zeros_like(traces)
    wide = [jnp.where(offset == o, traces, none) for o in range(OB)]
    corrected = jnp.dot(
        jnp.concatenate(wide, axis=1), map_ref[...], preferred_element_type=F32
    )
    groups = len(part_refs)
    owned = MBLK // groups
    ahead = (target // owned - lax.axis_index("grp") + groups) % groups
    place = ahead * owned + target % owned
    row = lax.broadcasted_iota(jnp.int32, (count, MBLK * rows), 0) % rows
    column = lax.broadcasted_iota(jnp.int32, (count, MBLK * rows), 1)
    chosen = one_hot((place == column // rows) & (row == column % rows))
    total = None
    for _ in range(3):
        part = corrected.astype(BF16)
        corrected = corrected - part.astype(F32)
        term = lax.dot_general(chosen, part, (((0,), (0,)), ((), ())), preferred_element_type=F32)
        total = term if total is None else total + term
    for number, ref in enumerate(part_refs):
        part = total[number * owned * rows : (number + 1) * owned * rows]
        ref[...] = part.reshape(ref.shape)


def stack(came, moveout_maps, groups):
    rows = came.shape[1] * BLK // (SH * RD)
    part = jax.ShapeDtypeStruct((MBLK // groups, rows, NT), F32)
    return pl.pallas_call(
        stack_body,
        out_shape=(part,) * groups,
        compiler_params=pltpu.CompilerParams(vmem_limit_bytes=40 << 20),
        name="stack",
    )(came, moveout_maps.reshape(OB * NT, NT))


def on_device(
    shot_data, weight_first, weight_middle, weight_last, moveout_maps, block_offset, block_target
):
    tiles, groups = lax.axis_size("tile"), lax.axis_size("grp")
    (own, weight_first, weight_middle, weight_last, block_offset, block_target) = (
        pltpu.with_memory_space_constraint(a, pltpu.HBM)
        for a in (
            shot_data,
            weight_first,
            weight_middle.reshape(9 * CH, CH),
            weight_last,
            block_offset,
            block_target.reshape(-1),
        )
    )
    low = lax.ppermute(shot_data, "tile", [(i, i + 1) for i in range(tiles - 1)])
    high = lax.ppermute(shot_data, "tile", [(i + 1, i) for i in range(tiles - 1)])
    *weights, split, slots = prepare(weight_first, weight_middle, weight_last, own)
    denoised, sent = denoise(block_offset, block_target, low, high, slots, *weights, split)
    came = lax.all_to_all(sent, "tile", 0, 0, tiled=True)
    stacked, *parts = stack(came, moveout_maps, groups)
    for ahead, part in enumerate(parts, 1):
        route = [(g, (g + ahead) % groups) for g in range(groups)]
        stacked = stacked + lax.ppermute(part, "grp", route)
    return denoised, stacked


def solution(mesh):
    in_specs = (
        P("grp", "tile", None),
        P(),
        P(),
        P(),
        P(),
        P(("grp", "tile")),
        P(("grp", "tile"), None),
    )
    out_specs = (P("grp", "tile", None), P("grp", "tile", None))
    return jax.shard_map(
        on_device, mesh=mesh, in_specs=in_specs, out_specs=out_specs, check_vma=False
    )
```

```python
import jax
import jax.numpy as jnp
from jax import lax
from jax.experimental import pallas as pl
from jax.experimental.pallas import tpu as pltpu
from jax.sharding import PartitionSpec as P

CH = 64
RD = 8
SH = 32
NT = 512
OB = 8
BLK = 128
MBLK = 32
LANES = 128
UNIT = 256
UNITS = 2
HALF = NT // 2
OUTER = RD + 4
INNER = RD + 2
EDGE = 3
SIDE = 16
F32 = jnp.float32
BF16 = jnp.bfloat16


def at_lane(shape, lane):
    return lax.broadcasted_iota(jnp.int32, shape, 1) % HALF == lane


def delayed(rows):
    return jnp.where(at_lane(rows.shape, 0), jnp.zeros_like(rows), pltpu.roll(rows, 1, 1))


def advanced(rows):
    last = rows.shape[1] - 1
    return jnp.where(at_lane(rows.shape, HALF - 1), jnp.zeros_like(rows), pltpu.roll(rows, last, 1))


def one_hot(condition):
    return condition.astype(F32).astype(BF16)


def prepare_body(tap1_ref, tap2_ref, tap3_ref, own_ref, first_ref, middle_ref, last_ref, split_ref, slots_ref, wide):
    tile = lax.axis_index("tile")
    low = (tile > 0).astype(F32)
    high = (tile < lax.axis_size("tile") - 1).astype(F32)

    shape = (9, UNIT)
    tap = lax.broadcasted_iota(jnp.int32, shape, 0)
    column = lax.broadcasted_iota(jnp.int32, shape, 1)
    inner = column - SIDE
    outer = inner - 4 * RD
    is_low, is_own = column < SIDE, inner < 4 * RD
    across = jnp.where(is_low, column % 4, jnp.where(is_own, inner % RD + EDGE, outer % 4 + EDGE + RD))
    delay = jnp.where(is_low, column // 4, jnp.where(is_own, inner // RD, outer // 4))
    used = (column < 2 * SIDE + 4 * RD) & ((is_low & (column % 4 < EDGE)) | (inner >= 0) & (is_own | (outer % 4 < EDGE)))
    for receiver in range(OUTER):
        inside = low if receiver < 2 else high if receiver >= OUTER - 2 else None
        for phase in range(2):
            a, d = across - receiver, delay - phase
            place = (tap == 3 * a + d) & (a >= 0) & (a <= 2) & (d >= 0) & (d <= 2) & used
            place = place.astype(F32)
            if inside is not None:
                place = place * inside
            block = lax.dot_general(
                tap1_ref[...], place.astype(BF16), (((0,), (0,)), ((), ())), preferred_element_type=F32
            )
            row = (2 * receiver + phase) * CH
            first_ref[row : row + CH, :] = block.astype(BF16)

    none = jnp.zeros((CH, CH), BF16)
    for across in range(3):
        taps = [tap2_ref[(3 * across + d) * CH : (3 * across + d + 1) * CH, :] for d in range(3)]
        lanes = slice(across * UNIT, (across + 1) * UNIT)
        middle_ref[:CH, lanes] = jnp.concatenate([*taps, none], axis=1)
        middle_ref[CH:, lanes] = jnp.concatenate([none, *taps], axis=1)

    none = jnp.zeros((1, CH), F32)
    taps = [tap3_ref[k : k + 1, :].astype(F32) for k in range(9)]
    kinds = [
        [taps[3 * a + 1] for a in range(3)], [taps[3 * a + 2] for a in range(3)],
        [taps[3 * a] for a in range(3)], [taps[3 * a + 1] for a in range(3)],
        [none] * 3, [taps[3 * a] for a in range(3)],
        [taps[3 * a + 2] for a in range(3)], [none] * 3,
    ]
    wide[...] = jnp.zeros_like(wide)
    for kind in range(4):
        row = [t for pair in zip(kinds[2 * kind], kinds[2 * kind + 1]) for t in pair]
        row = jnp.concatenate(row, axis=1)
        for receiver in range(RD):
            at = kind * RD + receiver
            wide[at : at + 1, receiver * 2 * CH : (receiver + 3) * 2 * CH] = row
    wide[:, : 2 * CH] = wide[:, : 2 * CH] * low
    wide[:, (INNER - 1) * 2 * CH :] = wide[:, (INNER - 1) * 2 * CH :] * high
    last_ref[...] = wide[...].astype(BF16)

    time = lax.broadcasted_iota(jnp.int32, (NT, 4 * HALF), 0)
    lane = lax.broadcasted_iota(jnp.int32, (NT, 4 * HALF), 1)
    split = one_hot(time == 2 * (lane % HALF) + lane // HALF - 1)
    split_ref[...] = split
    shots = own_ref.shape[0]
    taken = jnp.dot(own_ref[...].reshape(shots * RD, NT), split, preferred_element_type=F32)
    parts = [taken[:, s * HALF : (s + 1) * HALF].reshape(shots, RD, HALF) for s in range(4)]
    slots_ref[...] = jnp.concatenate(parts, axis=1).astype(BF16)


def prepare(weight_first, weight_middle, weight_last, own):
    shapes = (
        (OUTER * 2 * CH, UNIT),
        (2 * CH, 3 * UNIT),
        (4 * RD, INNER * 2 * CH),
        (NT, 4 * HALF),
        (own.shape[0], 4 * RD, HALF),
    )
    return pl.pallas_call(
        prepare_body,
        out_shape=tuple(jax.ShapeDtypeStruct(s, BF16) for s in shapes),
        scratch_shapes=[pltpu.VMEM(shapes[2], F32)],
        compiler_params=pltpu.CompilerParams(vmem_limit_bytes=24 << 20),
        name="prepare",
    )(weight_first, weight_middle, weight_last, own)


def product(accs, lhs, rhs, use):
    rows, depth = lhs.shape
    for n in range(rhs.shape[1] // UNIT):
        held = accs[n % UNITS]
        for k in range(depth // UNIT):
            piece = rhs[k * UNIT : (k + 1) * UNIT, n * UNIT : (n + 1) * UNIT]
            pltpu.matmul_push_rhs(piece, k % 2, n % UNITS)
            for c in range(rows // BLK):
                piece = lhs[c * BLK : (c + 1) * BLK, k * UNIT : (k + 1) * UNIT]
                pltpu.matmul_acc_lhs(held[c], piece, load_staged_rhs=k % 2 if c == 0 else None)
        for c in range(rows // BLK):
            use(n, c, pltpu.matmul_pop(held[c]))


def run(jobs):
    def push(number):
        for unit in range(UNITS):
            pltpu.matmul_push_rhs(jobs[number][0](unit), number % 2, unit)

    push(0)
    for number, (_, products, after) in enumerate(jobs):
        if number + 1 < len(jobs):
            push(number + 1)
        for n, (acc, lhs) in enumerate(products):
            for unit in range(UNITS):
                staged = number % 2 if n == 0 else None
                pltpu.matmul_acc_lhs(acc(unit), lhs(), load_staged_rhs=staged)
        for act in after:
            act()


def denoise_loop(
    offset_ref, target_ref, low_ref, high_ref, own, first_ref, middle_ref, last_ref, split_ref,
    denoised_ref, sent_ref, low, high, h1_even, h1_odd, h2_even, h2_odd, cleaned, rows4, accs,
):
    shots = own.shape[0]
    pairs = shots // UNITS
    per_block = BLK // RD

    for ref, held in ((low_ref, low), (high_ref, high)):
        def put(slot, c, part, held=held):
            for row in range(4):
                at = pl.ds(slot * 4 + row, shots, stride=SIDE)
                for half in range(HALF // LANES):
                    lanes = slice(half * LANES, (half + 1) * LANES)
                    held[half, at, :] = part[row * shots : (row + 1) * shots, lanes]

        edge = ref[...].reshape(EDGE * shots, NT)
        rest = jnp.zeros((BLK - EDGE * shots, NT), BF16)
        product(accs, jnp.concatenate([edge, rest], axis=0), split_ref, put)

    def taps(pair):
        def right(unit):
            shot = pair * UNITS + unit
            rows = pl.ds(pl.multiple_of(shot * SIDE, SIDE), SIDE)
            rest = jnp.zeros((UNIT - 4 * RD - 2 * SIDE, HALF), BF16)
            sides = [
                jnp.concatenate([side[0, rows, :], side[1, rows, :]], axis=1).astype(BF16)
                for side in (low, high)
            ]
            return jnp.concatenate([sides[0], own[shot], sides[1], rest], axis=0)

        return right

    def first_done(h1, receiver):
        def act():
            for unit in range(UNITS):
                both = jnp.maximum(pltpu.matmul_pop(accs[unit][receiver % 3]), 0.0).astype(BF16)
                h1[unit, receiver, CH : 3 * CH, :] = both
                h1[unit, receiver, :CH, :] = delayed(both[CH:])
                h1[unit, receiver, 3 * CH :, :] = advanced(both[:CH])

        return act

    def middle_done(h2, receiver):
        def act():
            for unit in range(UNITS):
                both = jnp.maximum(pltpu.matmul_pop(accs[unit][3 + receiver % 4]), 0.0)
                h2[unit, receiver * 2 * CH : (receiver + 1) * 2 * CH, :] = both.astype(BF16)

        return act

    def last_done(pair):
        def act():
            for unit in range(UNITS):
                shot = pair * UNITS + unit
                parts = pltpu.matmul_pop(accs[unit][7])
                seen = own[shot].astype(F32)
                rows = pl.ds(pl.multiple_of(shot * RD, RD), RD)
                even = parts[:RD] + delayed(parts[2 * RD : 3 * RD])
                odd = parts[RD : 2 * RD] + advanced(parts[3 * RD :])
                cleaned[rows, :HALF] = seen[RD : 2 * RD] - even
                cleaned[rows, HALF:] = seen[2 * RD : 3 * RD] - odd

        return act

    def first_job(pair, receivers):
        products = [
            (
                lambda unit, r=r: accs[unit][r % 3],
                lambda r=r: first_ref[r * 2 * CH : (r + 1) * 2 * CH, :],
            )
            for r in receivers
        ]
        return taps(pair), products, []

    def middle_job(h1, receiver):
        products = [
            (
                lambda unit, r=receiver - across: accs[unit][3 + r % 4],
                lambda across=across: middle_ref[:, across * UNIT : (across + 1) * UNIT],
            )
            for across in (2, 1, 0)
            if 0 <= receiver - across < INNER
        ]
        return lambda unit: h1[unit, receiver], products, []

    def last_job(h2, number):
        lanes = slice(number * UNIT, (number + 1) * UNIT)
        products = [(lambda unit: accs[unit][7], lambda: last_ref[:, lanes])]
        return lambda unit: h2[unit, lanes, :], products, []

    def stage(now, later, before):
        jobs = []
        for r in range(OUTER):
            if later and r % 3 == 0:
                jobs.append(first_job(later[0], range(r, r + 3)))
            if now:
                jobs.append(middle_job(now[0], r))
            if later:
                jobs[-1][2].append(first_done(later[1], r))
            if now and r >= 3:
                jobs[-1][2].append(middle_done(now[1], r - 3))
            if before and r % 2 == 1 and r < INNER:
                jobs.append(last_job(before[1], r // 2))
            if before and r == INNER:
                jobs[-1][2].append(last_done(before[0]))
        return jobs, [middle_done(now[1], INNER - 1)] if now else []

    def chain(*stages):
        jobs, tail = [], []
        for more, end in stages:
            more[0][2].extend(tail)
            jobs, tail = jobs + more, end
        jobs[-1][2].extend(tail)
        run(jobs)

    chain(stage(None, (0, h1_even), None))
    chain(stage((h1_even, h2_even), (1, h1_odd), None))

    def two(step, carry):
        pair = 2 * step + 1
        chain(
            stage((h1_odd, h2_odd), (pair + 1, h1_even), (pair - 1, h2_even)),
            stage((h1_even, h2_even), (pair + 2, h1_odd), (pair, h2_odd)),
        )
        return carry

    lax.fori_loop(0, (pairs - 2) // 2, two, 0)
    chain(stage((h1_odd, h2_odd), None, (pairs - 2, h2_even)))
    chain(([last_job(h2_odd, n) for n in range(INNER // 2)], [last_done(pairs - 1)]))

    lane = lax.broadcasted_iota(jnp.int32, (NT, NT), 0)
    time = lax.broadcasted_iota(jnp.int32, (NT, NT), 1)
    merge = one_hot(time == 2 * (lane % HALF) + lane // HALF)
    owners = sent_ref.shape[0]
    kept = BLK // owners

    def put(n, c, part):
        lanes = slice(n * UNIT, (n + 1) * UNIT)
        shot = slice(c * per_block, (c + 1) * per_block)
        denoised_ref[shot, :, lanes] = part.astype(BF16).reshape(per_block, RD, UNIT)
        rows4[:, c * kept : (c + 1) * kept, lanes] = part.reshape(owners, kept, UNIT)

    product(accs, cleaned[...].astype(BF16), merge, put)
    shape = (owners, kept, LANES // 2)
    for c in range(shots * RD // BLK):
        rows4[:, c * kept : (c + 1) * kept, NT : NT + LANES // 2] = jnp.full(shape, target_ref[c].astype(F32))
        rows4[:, c * kept : (c + 1) * kept, NT + LANES // 2 :] = jnp.full(shape, offset_ref[c].astype(F32))
    sent_ref[...] = rows4[...].astype(BF16)


def denoise_body(*refs):
    pl.run_scoped(
        lambda *accs: denoise_loop(*refs, (accs[:8], accs[8:])),
        *[
            pltpu.ACC(unit)((BLK if number < 7 else 4 * RD, UNIT), F32)
            for unit in range(UNITS)
            for number in range(8)
        ],
    )


def denoise(offsets, targets, low, high, slots, first, middle, last, split):
    shots, blocks = slots.shape[0], offsets.shape[0]
    owners = lax.axis_size("tile")
    sent = (owners, blocks * BLK // owners, NT + LANES)
    scalars = pl.BlockSpec(memory_space=pltpu.SMEM)
    whole = pl.BlockSpec(memory_space=pltpu.VMEM)
    macs = shots * RD * NT * CH * (9 * CH + 18)
    return pl.pallas_call(
        denoise_body,
        out_shape=(jax.ShapeDtypeStruct((shots, RD, NT), BF16), jax.ShapeDtypeStruct(sent, BF16)),
        in_specs=[scalars] * 2 + [whole] * 7,
        out_specs=(whole, whole),
        scratch_shapes=[pltpu.VMEM((HALF // LANES, shots * SIDE, LANES), F32)] * 2
        + [pltpu.VMEM((UNITS, OUTER, UNIT, HALF), BF16)] * 2
        + [pltpu.VMEM((UNITS, INNER * 2 * CH, HALF), BF16)] * 2
        + [pltpu.VMEM((shots * RD, NT), F32), pltpu.VMEM(sent, F32)],
        compiler_params=pltpu.CompilerParams(vmem_limit_bytes=40 << 20),
        cost_estimate=pl.CostEstimate(flops=2 * macs, transcendentals=0, bytes_accessed=4 << 20),
        name="denoise",
    )(offsets, targets, low, high, slots, first, middle, last, split)


def stack_body(came_ref, map_ref, *part_refs):
    tiles, kept, _ = came_ref.shape
    rows = kept * BLK // (SH * RD)
    count = tiles * kept
    came = came_ref[...].reshape(count, NT + LANES)
    target = came[:, NT : NT + 1].astype(F32).astype(jnp.int32)
    offset = came[:, NT + LANES // 2 : NT + LANES // 2 + 1].astype(F32)
    traces = came[:, :NT]
    none = jnp.zeros_like(traces)
    wide = [jnp.where(offset == o, traces, none) for o in range(OB)]
    corrected = jnp.dot(
        jnp.concatenate(wide, axis=1), map_ref[...], preferred_element_type=F32
    )
    owned = part_refs[0].shape[0]
    apart = (target // owned) ^ lax.axis_index("grp")
    order = jnp.where(apart == 0, 0, jnp.where(apart == 3, 1, apart + 1))
    place = order * owned + target % owned
    row = lax.broadcasted_iota(jnp.int32, (count, MBLK * rows), 0) % rows
    column = lax.broadcasted_iota(jnp.int32, (count, MBLK * rows), 1)
    chosen = one_hot((place == column // rows) & (row == column % rows))
    total = None
    for _ in range(3):
        part = corrected.astype(BF16)
        corrected = corrected - part.astype(F32)
        term = lax.dot_general(chosen, part, (((0,), (0,)), ((), ())), preferred_element_type=F32)
        total = term if total is None else total + term
    start = 0
    for ref in part_refs:
        end = start + ref.shape[0] * rows
        ref[...] = total[start:end].reshape(ref.shape)
        start = end


def stack(came, moveout_maps, groups):
    rows = came.shape[1] * BLK // (SH * RD)
    owned = MBLK // groups
    return pl.pallas_call(
        stack_body,
        out_shape=tuple(
            jax.ShapeDtypeStruct((n * owned, rows, NT), F32) for n in (1, 1, 2)
        ),
        compiler_params=pltpu.CompilerParams(vmem_limit_bytes=40 << 20),
        name="stack",
    )(came, moveout_maps.reshape(OB * NT, NT))


def edges(own):
    return own[:, -EDGE:, :].transpose(1, 0, 2), own[:, :EDGE, :].transpose(1, 0, 2)


def on_device(
    shot_data, weight_first, weight_middle, weight_last, moveout_maps, block_offset, block_target
):
    tiles, groups = lax.axis_size("tile"), lax.axis_size("grp")
    (own, weight_first, weight_middle, weight_last, block_offset, block_target) = (
        pltpu.with_memory_space_constraint(a, pltpu.HBM)
        for a in (
            shot_data,
            weight_first,
            weight_middle.reshape(9 * CH, CH),
            weight_last,
            block_offset,
            block_target.reshape(-1),
        )
    )
    low, high = edges(shot_data)
    low = lax.ppermute(low, "tile", [(i, i + 1) for i in range(tiles - 1)])
    high = lax.ppermute(high, "tile", [(i + 1, i) for i in range(tiles - 1)])
    *weights, split, slots = prepare(weight_first, weight_middle, weight_last, own)
    denoised, sent = denoise(block_offset, block_target, low, high, slots, *weights, split)
    came = lax.all_to_all(sent, "tile", 0, 0, tiled=True)
    kept, far, near = stack(came, moveout_maps, groups)
    near = lax.ppermute(near, "grp", [(g, g ^ 1) for g in range(groups)])
    owned = kept.shape[0]
    far = lax.ppermute(far + near[owned:], "grp", [(g, g ^ 3) for g in range(groups)])
    return denoised, kept + near[:owned] + far


def solution(mesh):
    in_specs = (
        P("grp", "tile", None),
        P(),
        P(),
        P(),
        P(),
        P(("grp", "tile")),
        P(("grp", "tile"), None),
    )
    out_specs = (P("grp", "tile", None), P("grp", "tile", None))
    return jax.shard_map(
        on_device, mesh=mesh, in_specs=in_specs, out_specs=out_specs, check_vma=False
    )
```

```python
import jax
import jax.numpy as jnp
from jax import lax
from jax.experimental import pallas as pl
from jax.experimental.pallas import tpu as pltpu
from jax.sharding import PartitionSpec as P

CH = 64
RD = 8
SH = 32
NT = 512
OB = 8
BLK = 128
MBLK = 32
LANES = 128
UNIT = 256
UNITS = 2
HALF = NT // 2
OUTER = RD + 4
INNER = RD + 2
EDGE = 3
SIDE = 16
F32 = jnp.float32
BF16 = jnp.bfloat16


def at_lane(shape, lane):
    return lax.broadcasted_iota(jnp.int32, shape, 1) % HALF == lane


def delayed(rows):
    return jnp.where(at_lane(rows.shape, 0), jnp.zeros_like(rows), pltpu.roll(rows, 1, 1))


def advanced(rows):
    last = rows.shape[1] - 1
    return jnp.where(at_lane(rows.shape, HALF - 1), jnp.zeros_like(rows), pltpu.roll(rows, last, 1))


def one_hot(condition):
    return condition.astype(F32).astype(BF16)


def prepare_body(tap1_ref, tap2_ref, tap3_ref, own_ref, first_ref, middle_ref, last_ref, split_ref, slots_ref, wide):
    tile = lax.axis_index("tile")
    low = (tile > 0).astype(F32)
    high = (tile < lax.axis_size("tile") - 1).astype(F32)

    shape = (9, UNIT)
    tap = lax.broadcasted_iota(jnp.int32, shape, 0)
    column = lax.broadcasted_iota(jnp.int32, shape, 1)
    inner = column - SIDE
    outer = inner - 4 * RD
    is_near, is_own = column < SIDE, inner < 4 * RD
    odd = tile % 2
    near, far = (EDGE + RD) * (1 - odd), (EDGE + RD) * odd
    across = jnp.where(is_near, column % 4 + near, jnp.where(is_own, inner % RD + EDGE, outer % 4 + far))
    delay = jnp.where(is_near, column // 4, jnp.where(is_own, inner // RD, outer // 4))
    used = (column < 2 * SIDE + 4 * RD) & ((is_near | (inner >= 4 * RD)) & (column % 4 < EDGE) | (inner >= 0) & is_own)
    for receiver in range(OUTER):
        inside = low if receiver < 2 else high if receiver >= OUTER - 2 else None
        for phase in range(2):
            a, d = across - receiver, delay - phase
            place = (tap == 3 * a + d) & (a >= 0) & (a <= 2) & (d >= 0) & (d <= 2) & used
            place = place.astype(F32)
            if inside is not None:
                place = place * inside
            block = lax.dot_general(
                tap1_ref[...], place.astype(BF16), (((0,), (0,)), ((), ())), preferred_element_type=F32
            )
            row = (2 * receiver + phase) * CH
            first_ref[row : row + CH, :] = block.astype(BF16)

    none = jnp.zeros((CH, CH), BF16)
    for across in range(3):
        taps = [tap2_ref[(3 * across + d) * CH : (3 * across + d + 1) * CH, :] for d in range(3)]
        lanes = slice(across * UNIT, (across + 1) * UNIT)
        middle_ref[:CH, lanes] = jnp.concatenate([*taps, none], axis=1)
        middle_ref[CH:, lanes] = jnp.concatenate([none, *taps], axis=1)

    none = jnp.zeros((1, CH), F32)
    taps = [tap3_ref[k : k + 1, :].astype(F32) for k in range(9)]
    kinds = [
        [taps[3 * a + 1] for a in range(3)], [taps[3 * a + 2] for a in range(3)],
        [taps[3 * a] for a in range(3)], [taps[3 * a + 1] for a in range(3)],
        [none] * 3, [taps[3 * a] for a in range(3)],
        [taps[3 * a + 2] for a in range(3)], [none] * 3,
    ]
    wide[...] = jnp.zeros_like(wide)
    for kind in range(4):
        row = [t for pair in zip(kinds[2 * kind], kinds[2 * kind + 1]) for t in pair]
        row = jnp.concatenate(row, axis=1)
        for receiver in range(RD):
            at = kind * RD + receiver
            wide[at : at + 1, receiver * 2 * CH : (receiver + 3) * 2 * CH] = row
    wide[:, : 2 * CH] = wide[:, : 2 * CH] * low
    wide[:, (INNER - 1) * 2 * CH :] = wide[:, (INNER - 1) * 2 * CH :] * high
    last_ref[...] = wide[...].astype(BF16)

    time = lax.broadcasted_iota(jnp.int32, (NT, 4 * HALF), 0)
    lane = lax.broadcasted_iota(jnp.int32, (NT, 4 * HALF), 1)
    split = one_hot(time == 2 * (lane % HALF) + lane // HALF - 1)
    split_ref[...] = split
    shots = own_ref.shape[0]
    taken = jnp.dot(own_ref[...].reshape(shots * RD, NT), split, preferred_element_type=F32)
    parts = [taken[:, s * HALF : (s + 1) * HALF].reshape(shots, RD, HALF) for s in range(4)]
    slots_ref[...] = jnp.concatenate(parts, axis=1).astype(BF16)


def prepare(weight_first, weight_middle, weight_last, own):
    shapes = (
        (OUTER * 2 * CH, UNIT),
        (2 * CH, 3 * UNIT),
        (4 * RD, INNER * 2 * CH),
        (NT, 4 * HALF),
        (own.shape[0], 4 * RD, HALF),
    )
    return pl.pallas_call(
        prepare_body,
        out_shape=tuple(jax.ShapeDtypeStruct(s, BF16) for s in shapes),
        scratch_shapes=[pltpu.VMEM(shapes[2], F32)],
        compiler_params=pltpu.CompilerParams(vmem_limit_bytes=24 << 20),
        name="prepare",
    )(weight_first, weight_middle, weight_last, own)


def product(accs, lhs, rhs, use):
    rows, depth = lhs.shape
    for n in range(rhs.shape[1] // UNIT):
        held = accs[n % UNITS]
        for k in range(depth // UNIT):
            piece = rhs[k * UNIT : (k + 1) * UNIT, n * UNIT : (n + 1) * UNIT]
            pltpu.matmul_push_rhs(piece, k % 2, n % UNITS)
            for c in range(rows // BLK):
                piece = lhs[c * BLK : (c + 1) * BLK, k * UNIT : (k + 1) * UNIT]
                pltpu.matmul_acc_lhs(held[c], piece, load_staged_rhs=k % 2 if c == 0 else None)
        for c in range(rows // BLK):
            use(n, c, pltpu.matmul_pop(held[c]))


def run(jobs):
    def push(number):
        for unit in range(UNITS):
            pltpu.matmul_push_rhs(jobs[number][0](unit), number % 2, unit)

    push(0)
    for number, (_, products, after) in enumerate(jobs):
        if number + 1 < len(jobs):
            push(number + 1)
        for n, (acc, lhs) in enumerate(products):
            for unit in range(UNITS):
                staged = number % 2 if n == 0 else None
                pltpu.matmul_acc_lhs(acc(unit), lhs(), load_staged_rhs=staged)
        for act in after:
            act()


def denoise_loop(
    offset_ref, target_ref, near_ref, far_ref, own, first_ref, middle_ref, last_ref, split_ref,
    denoised_ref, sent_ref, near, far, h1_even, h1_odd, h2_even, h2_odd, cleaned, rows4, accs,
):
    shots = own.shape[0]
    pairs = shots // UNITS
    per_block = BLK // RD

    for ref, held in ((near_ref, near), (far_ref, far)):
        def put(slot, c, part, held=held):
            for row in range(4):
                at = pl.ds(slot * 4 + row, shots, stride=SIDE)
                for half in range(HALF // LANES):
                    lanes = slice(half * LANES, (half + 1) * LANES)
                    held[half, at, :] = part[row * shots : (row + 1) * shots, lanes]

        edge = ref[...].reshape(EDGE * shots, NT)
        rest = jnp.zeros((BLK - EDGE * shots, NT), BF16)
        product(accs, jnp.concatenate([edge, rest], axis=0), split_ref, put)

    def taps(pair):
        def right(unit):
            shot = pair * UNITS + unit
            rows = pl.ds(pl.multiple_of(shot * SIDE, SIDE), SIDE)
            rest = jnp.zeros((UNIT - 4 * RD - 2 * SIDE, HALF), BF16)
            sides = [
                jnp.concatenate([side[0, rows, :], side[1, rows, :]], axis=1).astype(BF16)
                for side in (near, far)
            ]
            return jnp.concatenate([sides[0], own[shot], sides[1], rest], axis=0)

        return right

    def first_done(h1, receiver):
        def act():
            for unit in range(UNITS):
                both = jnp.maximum(pltpu.matmul_pop(accs[unit][receiver % 3]), 0.0).astype(BF16)
                h1[unit, receiver, CH : 3 * CH, :] = both
                h1[unit, receiver, :CH, :] = delayed(both[CH:])
                h1[unit, receiver, 3 * CH :, :] = advanced(both[:CH])

        return act

    def middle_done(h2, receiver):
        def act():
            for unit in range(UNITS):
                both = jnp.maximum(pltpu.matmul_pop(accs[unit][3 + receiver % 4]), 0.0)
                h2[unit, receiver * 2 * CH : (receiver + 1) * 2 * CH, :] = both.astype(BF16)

        return act

    def last_done(pair):
        def act():
            for unit in range(UNITS):
                shot = pair * UNITS + unit
                parts = pltpu.matmul_pop(accs[unit][7])
                seen = own[shot].astype(F32)
                rows = pl.ds(pl.multiple_of(shot * RD, RD), RD)
                even = parts[:RD] + delayed(parts[2 * RD : 3 * RD])
                odd = parts[RD : 2 * RD] + advanced(parts[3 * RD :])
                cleaned[rows, :HALF] = seen[RD : 2 * RD] - even
                cleaned[rows, HALF:] = seen[2 * RD : 3 * RD] - odd

        return act

    def first_job(pair, receivers):
        products = [
            (
                lambda unit, r=r: accs[unit][r % 3],
                lambda r=r: first_ref[r * 2 * CH : (r + 1) * 2 * CH, :],
            )
            for r in receivers
        ]
        return taps(pair), products, []

    def middle_job(h1, receiver):
        products = [
            (
                lambda unit, r=receiver - across: accs[unit][3 + r % 4],
                lambda across=across: middle_ref[:, across * UNIT : (across + 1) * UNIT],
            )
            for across in (2, 1, 0)
            if 0 <= receiver - across < INNER
        ]
        return lambda unit: h1[unit, receiver], products, []

    def last_job(h2, number):
        lanes = slice(number * UNIT, (number + 1) * UNIT)
        products = [(lambda unit: accs[unit][7], lambda: last_ref[:, lanes])]
        return lambda unit: h2[unit, lanes, :], products, []

    def stage(now, later, before):
        jobs = []
        for r in range(OUTER):
            if later and r % 3 == 0:
                jobs.append(first_job(later[0], range(r, r + 3)))
            if now:
                jobs.append(middle_job(now[0], r))
            if later:
                jobs[-1][2].append(first_done(later[1], r))
            if now and r >= 3:
                jobs[-1][2].append(middle_done(now[1], r - 3))
            if before and r % 2 == 1 and r < INNER:
                jobs.append(last_job(before[1], r // 2))
            if before and r == INNER:
                jobs[-1][2].append(last_done(before[0]))
        return jobs, [middle_done(now[1], INNER - 1)] if now else []

    def chain(*stages):
        jobs, tail = [], []
        for more, end in stages:
            more[0][2].extend(tail)
            jobs, tail = jobs + more, end
        jobs[-1][2].extend(tail)
        run(jobs)

    chain(stage(None, (0, h1_even), None))
    chain(stage((h1_even, h2_even), (1, h1_odd), None))

    def two(step, carry):
        pair = 2 * step + 1
        chain(
            stage((h1_odd, h2_odd), (pair + 1, h1_even), (pair - 1, h2_even)),
            stage((h1_even, h2_even), (pair + 2, h1_odd), (pair, h2_odd)),
        )
        return carry

    lax.fori_loop(0, (pairs - 2) // 2, two, 0)
    chain(stage((h1_odd, h2_odd), None, (pairs - 2, h2_even)))
    chain(([last_job(h2_odd, n) for n in range(INNER // 2)], [last_done(pairs - 1)]))

    lane = lax.broadcasted_iota(jnp.int32, (NT, NT), 0)
    time = lax.broadcasted_iota(jnp.int32, (NT, NT), 1)
    merge = one_hot(time == 2 * (lane % HALF) + lane // HALF)
    owners = sent_ref.shape[0]
    kept = BLK // owners

    def put(n, c, part):
        lanes = slice(n * UNIT, (n + 1) * UNIT)
        shot = slice(c * per_block, (c + 1) * per_block)
        denoised_ref[shot, :, lanes] = part.astype(BF16).reshape(per_block, RD, UNIT)
        rows4[:, c * kept : (c + 1) * kept, lanes] = part.reshape(owners, kept, UNIT)

    product(accs, cleaned[...].astype(BF16), merge, put)
    shape = (owners, kept, LANES // 2)
    for c in range(shots * RD // BLK):
        rows4[:, c * kept : (c + 1) * kept, NT : NT + LANES // 2] = jnp.full(shape, target_ref[c].astype(F32))
        rows4[:, c * kept : (c + 1) * kept, NT + LANES // 2 :] = jnp.full(shape, offset_ref[c].astype(F32))
    sent_ref[...] = rows4[...].astype(BF16)


def denoise_body(*refs):
    pl.run_scoped(
        lambda *accs: denoise_loop(*refs, (accs[:8], accs[8:])),
        *[
            pltpu.ACC(unit)((BLK if number < 7 else 4 * RD, UNIT), F32)
            for unit in range(UNITS)
            for number in range(8)
        ],
    )


def denoise(offsets, targets, near, far, slots, first, middle, last, split):
    shots, blocks = slots.shape[0], offsets.shape[0]
    owners = lax.axis_size("tile")
    sent = (owners, blocks * BLK // owners, NT + LANES)
    scalars = pl.BlockSpec(memory_space=pltpu.SMEM)
    whole = pl.BlockSpec(memory_space=pltpu.VMEM)
    macs = shots * RD * NT * CH * (9 * CH + 18)
    return pl.pallas_call(
        denoise_body,
        out_shape=(jax.ShapeDtypeStruct((shots, RD, NT), BF16), jax.ShapeDtypeStruct(sent, BF16)),
        in_specs=[scalars] * 2 + [whole] * 7,
        out_specs=(whole, whole),
        scratch_shapes=[pltpu.VMEM((HALF // LANES, shots * SIDE, LANES), F32)] * 2
        + [pltpu.VMEM((UNITS, OUTER, UNIT, HALF), BF16)] * 2
        + [pltpu.VMEM((UNITS, INNER * 2 * CH, HALF), BF16)] * 2
        + [pltpu.VMEM((shots * RD, NT), F32), pltpu.VMEM(sent, F32)],
        compiler_params=pltpu.CompilerParams(vmem_limit_bytes=40 << 20),
        cost_estimate=pl.CostEstimate(flops=2 * macs, transcendentals=0, bytes_accessed=4 << 20),
        name="denoise",
    )(offsets, targets, near, far, slots, first, middle, last, split)


def stack_body(came_ref, map_ref, *part_refs):
    tiles, kept, _ = came_ref.shape
    rows = kept * BLK // (SH * RD)
    count = tiles * kept
    came = came_ref[...].reshape(count, NT + LANES)
    target = came[:, NT : NT + 1].astype(F32).astype(jnp.int32)
    offset = came[:, NT + LANES // 2 : NT + LANES // 2 + 1].astype(F32)
    traces = came[:, :NT]
    none = jnp.zeros_like(traces)
    wide = [jnp.where(offset == o, traces, none) for o in range(OB)]
    corrected = jnp.dot(
        jnp.concatenate(wide, axis=1), map_ref[...], preferred_element_type=F32
    )
    groups = len(part_refs)
    owned = MBLK // groups
    place = ((target // owned) ^ lax.axis_index("grp")) * owned + target % owned
    row = lax.broadcasted_iota(jnp.int32, (count, MBLK * rows), 0) % rows
    column = lax.broadcasted_iota(jnp.int32, (count, MBLK * rows), 1)
    chosen = one_hot((place == column // rows) & (row == column % rows))
    total = None
    for _ in range(3):
        part = corrected.astype(BF16)
        corrected = corrected - part.astype(F32)
        term = lax.dot_general(chosen, part, (((0,), (0,)), ((), ())), preferred_element_type=F32)
        total = term if total is None else total + term
    for number, ref in enumerate(part_refs):
        part = total[number * owned * rows : (number + 1) * owned * rows]
        ref[...] = part.reshape(ref.shape)


def stack(came, moveout_maps, groups):
    rows = came.shape[1] * BLK // (SH * RD)
    part = jax.ShapeDtypeStruct((MBLK // groups, rows, NT), F32)
    return pl.pallas_call(
        stack_body,
        out_shape=(part,) * groups,
        compiler_params=pltpu.CompilerParams(vmem_limit_bytes=40 << 20),
        name="stack",
    )(came, moveout_maps.reshape(OB * NT, NT))


def edges(own):
    odd = lax.axis_index("tile") % 2 == 1
    start, end = own[:, :EDGE, :].transpose(1, 0, 2), own[:, -EDGE:, :].transpose(1, 0, 2)
    return jnp.where(odd, start, end), jnp.where(odd, end, start)


def on_device(
    shot_data, weight_first, weight_middle, weight_last, moveout_maps, block_offset, block_target
):
    tiles, groups = lax.axis_size("tile"), lax.axis_size("grp")
    (own, weight_first, weight_middle, weight_last, block_offset, block_target) = (
        pltpu.with_memory_space_constraint(a, pltpu.HBM)
        for a in (
            shot_data,
            weight_first,
            weight_middle.reshape(9 * CH, CH),
            weight_last,
            block_offset,
            block_target.reshape(-1),
        )
    )
    near, far = edges(shot_data)
    near = lax.ppermute(near, "tile", [(i, i ^ 1) for i in range(tiles)])
    pairs = [(i, i + 1) for i in range(1, tiles - 1, 2)]
    far = lax.ppermute(far, "tile", pairs + [(j, i) for i, j in pairs])
    *weights, split, slots = prepare(weight_first, weight_middle, weight_last, own)
    denoised, sent = denoise(block_offset, block_target, near, far, slots, *weights, split)
    came = lax.all_to_all(sent, "tile", 0, 0, tiled=True)
    stacked, *parts = stack(came, moveout_maps, groups)
    for apart, part in enumerate(parts, 1):
        stacked = stacked + lax.ppermute(part, "grp", [(g, g ^ apart) for g in range(groups)])
    return denoised, stacked


def solution(mesh):
    in_specs = (
        P("grp", "tile", None),
        P(),
        P(),
        P(),
        P(),
        P(("grp", "tile")),
        P(("grp", "tile"), None),
    )
    out_specs = (P("grp", "tile", None), P("grp", "tile", None))
    return jax.shard_map(
        on_device, mesh=mesh, in_specs=in_specs, out_specs=out_specs, check_vma=False
    )
```

```python
import jax
import jax.numpy as jnp
from jax import lax
from jax.experimental import pallas as pl
from jax.experimental.pallas import tpu as pltpu
from jax.sharding import PartitionSpec as P

CH = 64
RD = 8
SH = 32
NT = 512
OB = 8
BLK = 128
MBLK = 32
LANES = 128
UNIT = 256
UNITS = 2
HALF = NT // 2
OUTER = RD + 4
INNER = RD + 2
EDGE = 3
SIDE = 16
STAGES = 4
F32 = jnp.float32
BF16 = jnp.bfloat16


def at_lane(shape, lane):
    return lax.broadcasted_iota(jnp.int32, shape, 1) % HALF == lane


def delayed(rows):
    return jnp.where(at_lane(rows.shape, 0), jnp.zeros_like(rows), pltpu.roll(rows, 1, 1))


def advanced(rows):
    last = rows.shape[1] - 1
    return jnp.where(at_lane(rows.shape, HALF - 1), jnp.zeros_like(rows), pltpu.roll(rows, last, 1))


def one_hot(condition):
    return condition.astype(F32).astype(BF16)


def prepare_body(tap1_ref, tap2_ref, tap3_ref, own_ref, first_ref, middle_ref, last_ref, split_ref, slots_ref, wide):
    tile = lax.axis_index("tile")
    low = (tile > 0).astype(F32)
    high = (tile < lax.axis_size("tile") - 1).astype(F32)

    shape = (9, UNIT)
    tap = lax.broadcasted_iota(jnp.int32, shape, 0)
    column = lax.broadcasted_iota(jnp.int32, shape, 1)
    inner = column - SIDE
    outer = inner - 4 * RD
    is_near, is_own = column < SIDE, inner < 4 * RD
    odd = tile % 2
    near, far = (EDGE + RD) * (1 - odd), (EDGE + RD) * odd
    across = jnp.where(is_near, column % 4 + near, jnp.where(is_own, inner % RD + EDGE, outer % 4 + far))
    delay = jnp.where(is_near, column // 4, jnp.where(is_own, inner // RD, outer // 4))
    used = (column < 2 * SIDE + 4 * RD) & ((is_near | (inner >= 4 * RD)) & (column % 4 < EDGE) | (inner >= 0) & is_own)
    for receiver in range(OUTER):
        inside = low if receiver < 2 else high if receiver >= OUTER - 2 else None
        for phase in range(2):
            a, d = across - receiver, delay - phase
            place = (tap == 3 * a + d) & (a >= 0) & (a <= 2) & (d >= 0) & (d <= 2) & used
            place = place.astype(F32)
            if inside is not None:
                place = place * inside
            block = lax.dot_general(
                tap1_ref[...], place.astype(BF16), (((0,), (0,)), ((), ())), preferred_element_type=F32
            )
            row = (2 * receiver + phase) * CH
            first_ref[row : row + CH, :] = block.astype(BF16)

    none = jnp.zeros((CH, CH), BF16)
    for across in range(3):
        taps = [tap2_ref[(3 * across + d) * CH : (3 * across + d + 1) * CH, :] for d in range(3)]
        lanes = slice(across * UNIT, (across + 1) * UNIT)
        middle_ref[:CH, lanes] = jnp.concatenate([*taps, none], axis=1)
        middle_ref[CH:, lanes] = jnp.concatenate([none, *taps], axis=1)

    none = jnp.zeros((1, CH), F32)
    taps = [tap3_ref[k : k + 1, :].astype(F32) for k in range(9)]
    kinds = [
        [taps[3 * a + 1] for a in range(3)], [taps[3 * a + 2] for a in range(3)],
        [taps[3 * a] for a in range(3)], [taps[3 * a + 1] for a in range(3)],
        [none] * 3, [taps[3 * a] for a in range(3)],
        [taps[3 * a + 2] for a in range(3)], [none] * 3,
    ]
    wide[...] = jnp.zeros_like(wide)
    for kind in range(4):
        row = [t for pair in zip(kinds[2 * kind], kinds[2 * kind + 1]) for t in pair]
        row = jnp.concatenate(row, axis=1)
        for receiver in range(RD):
            at = kind * RD + receiver
            wide[at : at + 1, receiver * 2 * CH : (receiver + 3) * 2 * CH] = row
    wide[:, : 2 * CH] = wide[:, : 2 * CH] * low
    wide[:, (INNER - 1) * 2 * CH :] = wide[:, (INNER - 1) * 2 * CH :] * high
    last_ref[...] = wide[...].astype(BF16)

    time = lax.broadcasted_iota(jnp.int32, (NT, 4 * HALF), 0)
    lane = lax.broadcasted_iota(jnp.int32, (NT, 4 * HALF), 1)
    split = one_hot(time == 2 * (lane % HALF) + lane // HALF - 1)
    split_ref[...] = split
    shots = own_ref.shape[0]
    taken = jnp.dot(own_ref[...].reshape(shots * RD, NT), split, preferred_element_type=F32)
    parts = [taken[:, s * HALF : (s + 1) * HALF].reshape(shots, RD, HALF) for s in range(4)]
    slots_ref[...] = jnp.concatenate(parts, axis=1).astype(BF16)


def prepare(weight_first, weight_middle, weight_last, own):
    shapes = (
        (OUTER * 2 * CH, UNIT),
        (2 * CH, 3 * UNIT),
        (4 * RD, INNER * 2 * CH),
        (NT, 4 * HALF),
        (own.shape[0], 4 * RD, HALF),
    )
    return pl.pallas_call(
        prepare_body,
        out_shape=tuple(jax.ShapeDtypeStruct(s, BF16) for s in shapes),
        scratch_shapes=[pltpu.VMEM(shapes[2], F32)],
        compiler_params=pltpu.CompilerParams(vmem_limit_bytes=24 << 20),
        name="prepare",
    )(weight_first, weight_middle, weight_last, own)


def product(accs, lhs, rhs, use):
    rows, depth = lhs.shape
    for n in range(rhs.shape[1] // UNIT):
        held = accs[n % UNITS]
        for k in range(depth // UNIT):
            piece = rhs[k * UNIT : (k + 1) * UNIT, n * UNIT : (n + 1) * UNIT]
            pltpu.matmul_push_rhs(piece, k % 2, n % UNITS)
            for c in range(rows // BLK):
                piece = lhs[c * BLK : (c + 1) * BLK, k * UNIT : (k + 1) * UNIT]
                pltpu.matmul_acc_lhs(held[c], piece, load_staged_rhs=k % 2 if c == 0 else None)
        for c in range(rows // BLK):
            use(n, c, pltpu.matmul_pop(held[c]))


def run(jobs):
    def push(number):
        for unit in range(UNITS):
            pltpu.matmul_push_rhs(jobs[number][0](unit), number % 2, unit)

    push(0)
    for number, (_, products, after) in enumerate(jobs):
        if number + 1 < len(jobs):
            push(number + 1)
        for n, (acc, lhs) in enumerate(products):
            for unit in range(UNITS):
                staged = number % 2 if n == 0 else None
                pltpu.matmul_acc_lhs(acc(unit), lhs(), load_staged_rhs=staged)
        for act in after:
            act()


def denoise_loop(
    near_ref, far_ref, own, first_ref, middle_ref, last_ref, split_ref,
    denoised_ref, sent_ref, near, far, h1_even, h1_odd, h2_even, h2_odd, cleaned, rows4, accs,
):
    shots = own.shape[0]
    pairs = shots // UNITS
    per_block = BLK // RD

    for ref, held in ((near_ref, near), (far_ref, far)):
        def put(slot, c, part, held=held):
            for row in range(4):
                at = pl.ds(slot * 4 + row, shots, stride=SIDE)
                for half in range(HALF // LANES):
                    lanes = slice(half * LANES, (half + 1) * LANES)
                    held[half, at, :] = part[row * shots : (row + 1) * shots, lanes]

        edge = ref[...].reshape(EDGE * shots, NT)
        rest = jnp.zeros((BLK - EDGE * shots, NT), BF16)
        product(accs, jnp.concatenate([edge, rest], axis=0), split_ref, put)

    def taps(pair):
        def right(unit):
            shot = pair * UNITS + unit
            rows = pl.ds(pl.multiple_of(shot * SIDE, SIDE), SIDE)
            rest = jnp.zeros((UNIT - 4 * RD - 2 * SIDE, HALF), BF16)
            sides = [
                jnp.concatenate([side[0, rows, :], side[1, rows, :]], axis=1).astype(BF16)
                for side in (near, far)
            ]
            return jnp.concatenate([sides[0], own[shot], sides[1], rest], axis=0)

        return right

    def first_done(h1, receiver):
        def act():
            for unit in range(UNITS):
                both = jnp.maximum(pltpu.matmul_pop(accs[unit][receiver % 3]), 0.0).astype(BF16)
                h1[unit, receiver, CH : 3 * CH, :] = both
                h1[unit, receiver, :CH, :] = delayed(both[CH:])
                h1[unit, receiver, 3 * CH :, :] = advanced(both[:CH])

        return act

    def middle_done(h2, receiver):
        def act():
            for unit in range(UNITS):
                both = jnp.maximum(pltpu.matmul_pop(accs[unit][3 + receiver % 4]), 0.0)
                h2[unit, receiver * 2 * CH : (receiver + 1) * 2 * CH, :] = both.astype(BF16)

        return act

    def last_done(pair):
        def act():
            for unit in range(UNITS):
                shot = pair * UNITS + unit
                parts = pltpu.matmul_pop(accs[unit][7])
                seen = own[shot].astype(F32)
                rows = pl.ds(pl.multiple_of(shot * RD, RD), RD)
                even = parts[:RD] + delayed(parts[2 * RD : 3 * RD])
                odd = parts[RD : 2 * RD] + advanced(parts[3 * RD :])
                cleaned[rows, :HALF] = seen[RD : 2 * RD] - even
                cleaned[rows, HALF:] = seen[2 * RD : 3 * RD] - odd

        return act

    def first_job(pair, receivers):
        products = [
            (
                lambda unit, r=r: accs[unit][r % 3],
                lambda r=r: first_ref[r * 2 * CH : (r + 1) * 2 * CH, :],
            )
            for r in receivers
        ]
        return taps(pair), products, []

    def middle_job(h1, receiver):
        products = [
            (
                lambda unit, r=receiver - across: accs[unit][3 + r % 4],
                lambda across=across: middle_ref[:, across * UNIT : (across + 1) * UNIT],
            )
            for across in (2, 1, 0)
            if 0 <= receiver - across < INNER
        ]
        return lambda unit: h1[unit, receiver], products, []

    def last_job(h2, number):
        lanes = slice(number * UNIT, (number + 1) * UNIT)
        products = [(lambda unit: accs[unit][7], lambda: last_ref[:, lanes])]
        return lambda unit: h2[unit, lanes, :], products, []

    def stage(now, later, before):
        jobs = []
        for r in range(OUTER):
            if later and r % 3 == 0:
                jobs.append(first_job(later[0], range(r, r + 3)))
            if now:
                jobs.append(middle_job(now[0], r))
            if later:
                jobs[-1][2].append(first_done(later[1], r))
            if now and r >= 3:
                jobs[-1][2].append(middle_done(now[1], r - 3))
            if before and r % 2 == 1 and r < INNER:
                jobs.append(last_job(before[1], r // 2))
            if before and r == INNER:
                jobs[-1][2].append(last_done(before[0]))
        return jobs, [middle_done(now[1], INNER - 1)] if now else []

    def chain(*stages):
        jobs, tail = [], []
        for more, end in stages:
            more[0][2].extend(tail)
            jobs, tail = jobs + more, end
        jobs[-1][2].extend(tail)
        run(jobs)

    buffers = ((h1_even, h2_even), (h1_odd, h2_odd))

    def full(pair, parity):
        now, other = buffers[parity], buffers[1 - parity]
        return stage(now, (pair + 1, other[0]), (pair - 1, other[1]))

    def several(step, carry):
        pair = STAGES * step + 1
        chain(*[full(pair + n, (n + 1) % 2) for n in range(STAGES)])
        return carry

    chain(stage(None, (0, h1_even), None), stage(buffers[0], (1, h1_odd), None))
    steps = (pairs - 2) // STAGES
    lax.fori_loop(0, steps, several, 0)
    rest = [full(pair, pair % 2) for pair in range(STAGES * steps + 1, pairs - 1)]
    end = [last_job(h2_odd, n) for n in range(INNER // 2)], [last_done(pairs - 1)]
    chain(*rest, stage(buffers[1], None, (pairs - 2, h2_even)), end)

    lane = lax.broadcasted_iota(jnp.int32, (NT, NT), 0)
    time = lax.broadcasted_iota(jnp.int32, (NT, NT), 1)
    merge = one_hot(time == 2 * (lane % HALF) + lane // HALF)
    owners = sent_ref.shape[0]
    kept = BLK // owners

    def put(n, c, part):
        lanes = slice(n * UNIT, (n + 1) * UNIT)
        shot = slice(c * per_block, (c + 1) * per_block)
        denoised_ref[shot, :, lanes] = part.astype(BF16).reshape(per_block, RD, UNIT)
        rows4[:, c * kept : (c + 1) * kept, lanes] = part.reshape(owners, kept, UNIT)

    product(accs, cleaned[...].astype(BF16), merge, put)
    sent_ref[...] = rows4[...].astype(BF16)


def denoise_body(*refs):
    pl.run_scoped(
        lambda *accs: denoise_loop(*refs, (accs[:8], accs[8:])),
        *[
            pltpu.ACC(unit)((BLK if number < 7 else 4 * RD, UNIT), F32)
            for unit in range(UNITS)
            for number in range(8)
        ],
    )


def denoise(near, far, slots, first, middle, last, split):
    shots = slots.shape[0]
    owners = lax.axis_size("tile")
    sent = (owners, shots * RD // owners, NT)
    whole = pl.BlockSpec(memory_space=pltpu.VMEM)
    macs = shots * RD * NT * CH * (9 * CH + 18)
    return pl.pallas_call(
        denoise_body,
        out_shape=(jax.ShapeDtypeStruct((shots, RD, NT), BF16), jax.ShapeDtypeStruct(sent, BF16)),
        in_specs=[whole] * 7,
        out_specs=(whole, whole),
        scratch_shapes=[pltpu.VMEM((HALF // LANES, shots * SIDE, LANES), F32)] * 2
        + [pltpu.VMEM((UNITS, OUTER, UNIT, HALF), BF16)] * 2
        + [pltpu.VMEM((UNITS, INNER * 2 * CH, HALF), BF16)] * 2
        + [pltpu.VMEM((shots * RD, NT), F32), pltpu.VMEM(sent, F32)],
        compiler_params=pltpu.CompilerParams(vmem_limit_bytes=40 << 20),
        cost_estimate=pl.CostEstimate(flops=2 * macs, transcendentals=0, bytes_accessed=4 << 20),
        name="denoise",
    )(near, far, slots, first, middle, last, split)


def stack_body(came_ref, choice_ref, map_ref, *part_refs):
    tiles, kept, _ = came_ref.shape
    rows = kept * BLK // (SH * RD)
    count = tiles * kept
    traces = came_ref[...].reshape(count, NT)
    blocks = kept // rows
    choice = [
        jnp.concatenate(
            [
                jnp.broadcast_to(choice_ref[:, n : n + 1, :], (tiles, rows, LANES))
                for n in range(start, start + blocks)
            ],
            axis=1,
        ).reshape(count, LANES)[:, :1]
        for start in (0, blocks)
    ]
    target, offset = choice[0].astype(jnp.int32), choice[1]
    none = jnp.zeros_like(traces)
    wide = [jnp.where(offset == o, traces, none) for o in range(OB)]
    corrected = jnp.dot(
        jnp.concatenate(wide, axis=1), map_ref[...], preferred_element_type=F32
    )
    groups = len(part_refs)
    owned = MBLK // groups
    place = ((target // owned) ^ lax.axis_index("grp")) * owned + target % owned
    row = lax.broadcasted_iota(jnp.int32, (count, MBLK * rows), 0) % rows
    column = lax.broadcasted_iota(jnp.int32, (count, MBLK * rows), 1)
    chosen = one_hot((place == column // rows) & (row == column % rows))
    total = None
    for _ in range(3):
        part = corrected.astype(BF16)
        corrected = corrected - part.astype(F32)
        term = lax.dot_general(chosen, part, (((0,), (0,)), ((), ())), preferred_element_type=F32)
        total = term if total is None else total + term
    for number, ref in enumerate(part_refs):
        part = total[number * owned * rows : (number + 1) * owned * rows]
        ref[...] = part.reshape(ref.shape)


def stack(came, choice, moveout_maps, groups):
    rows = came.shape[1] * BLK // (SH * RD)
    part = jax.ShapeDtypeStruct((MBLK // groups, rows, NT), F32)
    return pl.pallas_call(
        stack_body,
        out_shape=(part,) * groups,
        compiler_params=pltpu.CompilerParams(vmem_limit_bytes=40 << 20),
        name="stack",
    )(came, choice, moveout_maps.reshape(OB * NT, NT))


def edges(own):
    odd = lax.axis_index("tile") % 2 == 1
    start, end = own[:, :EDGE, :].transpose(1, 0, 2), own[:, -EDGE:, :].transpose(1, 0, 2)
    return jnp.where(odd, start, end), jnp.where(odd, end, start)


def on_device(
    shot_data, weight_first, weight_middle, weight_last, moveout_maps, block_offset, block_target
):
    tiles, groups = lax.axis_size("tile"), lax.axis_size("grp")
    (own, weight_first, weight_middle, weight_last) = (
        pltpu.with_memory_space_constraint(a, pltpu.HBM)
        for a in (
            shot_data,
            weight_first,
            weight_middle.reshape(9 * CH, CH),
            weight_last,
        )
    )
    choice = jnp.concatenate([block_target.reshape(-1), block_offset]).astype(F32)
    mine = jnp.arange(tiles)[:, None, None] == lax.axis_index("tile")
    choice = jnp.where(mine, choice[None, :, None], jnp.zeros((tiles, choice.shape[0], LANES), F32))
    choice = lax.psum(choice, "tile")
    near, far = edges(shot_data)
    near = lax.ppermute(near, "tile", [(i, i ^ 1) for i in range(tiles)])
    pairs = [(i, i + 1) for i in range(1, tiles - 1, 2)]
    far = lax.ppermute(far, "tile", pairs + [(j, i) for i, j in pairs])
    *weights, split, slots = prepare(weight_first, weight_middle, weight_last, own)
    denoised, sent = denoise(near, far, slots, *weights, split)
    sent, choice = lax.optimization_barrier((sent, choice))
    came = lax.all_to_all(sent, "tile", 0, 0, tiled=True)
    stacked, *parts = stack(came, choice, moveout_maps, groups)
    for apart in (2, 1, 3):
        part = lax.ppermute(parts[apart - 1], "grp", [(g, g ^ apart) for g in range(groups)])
        stacked = stacked + part
    return denoised, stacked


def solution(mesh):
    in_specs = (
        P("grp", "tile", None),
        P(),
        P(),
        P(),
        P(),
        P(("grp", "tile")),
        P(("grp", "tile"), None),
    )
    out_specs = (P("grp", "tile", None), P("grp", "tile", None))
    return jax.shard_map(
        on_device, mesh=mesh, in_specs=in_specs, out_specs=out_specs, check_vma=False
    )
```

```python
import jax
import jax.numpy as jnp
from jax import lax
from jax.experimental import pallas as pl
from jax.experimental.pallas import tpu as pltpu
from jax.sharding import PartitionSpec as P

CH = 64
RD = 8
SH = 32
NT = 512
OB = 8
BLK = 128
MBLK = 32
LANES = 128
UNIT = 256
UNITS = 2
HALF = NT // 2
OUTER = RD + 4
INNER = RD + 2
EDGE = 3
SIDE = 16
STAGES = 4
F32 = jnp.float32
BF16 = jnp.bfloat16


def at_lane(shape, lane):
    return lax.broadcasted_iota(jnp.int32, shape, 1) % HALF == lane


def delayed(rows):
    return jnp.where(at_lane(rows.shape, 0), jnp.zeros_like(rows), pltpu.roll(rows, 1, 1))


def advanced(rows):
    last = rows.shape[1] - 1
    return jnp.where(at_lane(rows.shape, HALF - 1), jnp.zeros_like(rows), pltpu.roll(rows, last, 1))


def one_hot(condition):
    return condition.astype(F32).astype(BF16)


def prepare_body(tap1_ref, tap2_ref, tap3_ref, own_ref, first_ref, middle_ref, last_ref, split_ref, slots_ref, wide):
    tile = lax.axis_index("tile")
    low = (tile > 0).astype(F32)
    high = (tile < lax.axis_size("tile") - 1).astype(F32)

    shape = (9, UNIT)
    tap = lax.broadcasted_iota(jnp.int32, shape, 0)
    column = lax.broadcasted_iota(jnp.int32, shape, 1)
    inner = column - SIDE
    outer = inner - 4 * RD
    is_near, is_own = column < SIDE, inner < 4 * RD
    odd = tile % 2
    near, far = (EDGE + RD) * (1 - odd), (EDGE + RD) * odd
    across = jnp.where(is_near, column % 4 + near, jnp.where(is_own, inner % RD + EDGE, outer % 4 + far))
    delay = jnp.where(is_near, column // 4, jnp.where(is_own, inner // RD, outer // 4))
    used = (column < 2 * SIDE + 4 * RD) & ((is_near | (inner >= 4 * RD)) & (column % 4 < EDGE) | (inner >= 0) & is_own)
    for receiver in range(OUTER):
        inside = low if receiver < 2 else high if receiver >= OUTER - 2 else None
        for phase in range(2):
            a, d = across - receiver, delay - phase
            place = (tap == 3 * a + d) & (a >= 0) & (a <= 2) & (d >= 0) & (d <= 2) & used
            place = place.astype(F32)
            if inside is not None:
                place = place * inside
            block = lax.dot_general(
                tap1_ref[...], place.astype(BF16), (((0,), (0,)), ((), ())), preferred_element_type=F32
            )
            row = (2 * receiver + phase) * CH
            first_ref[row : row + CH, :] = block.astype(BF16)

    none = jnp.zeros((CH, CH), BF16)
    for across in range(3):
        taps = [tap2_ref[(3 * across + d) * CH : (3 * across + d + 1) * CH, :] for d in range(3)]
        lanes = slice(across * UNIT, (across + 1) * UNIT)
        middle_ref[:CH, lanes] = jnp.concatenate([*taps, none], axis=1)
        middle_ref[CH:, lanes] = jnp.concatenate([none, *taps], axis=1)

    none = jnp.zeros((1, CH), F32)
    taps = [tap3_ref[k : k + 1, :].astype(F32) for k in range(9)]
    kinds = [
        [taps[3 * a + 1] for a in range(3)], [taps[3 * a + 2] for a in range(3)],
        [taps[3 * a] for a in range(3)], [taps[3 * a + 1] for a in range(3)],
        [none] * 3, [taps[3 * a] for a in range(3)],
        [taps[3 * a + 2] for a in range(3)], [none] * 3,
    ]
    wide[...] = jnp.zeros_like(wide)
    for kind in range(4):
        row = [t for pair in zip(kinds[2 * kind], kinds[2 * kind + 1]) for t in pair]
        row = jnp.concatenate(row, axis=1)
        for receiver in range(RD):
            at = kind * RD + receiver
            wide[at : at + 1, receiver * 2 * CH : (receiver + 3) * 2 * CH] = row
    wide[:, : 2 * CH] = wide[:, : 2 * CH] * low
    wide[:, (INNER - 1) * 2 * CH :] = wide[:, (INNER - 1) * 2 * CH :] * high
    last_ref[...] = wide[...].astype(BF16)

    time = lax.broadcasted_iota(jnp.int32, (NT, 4 * HALF), 0)
    lane = lax.broadcasted_iota(jnp.int32, (NT, 4 * HALF), 1)
    split = one_hot(time == 2 * (lane % HALF) + lane // HALF - 1)
    split_ref[...] = split
    shots = own_ref.shape[0]
    taken = jnp.dot(own_ref[...].reshape(shots * RD, NT), split, preferred_element_type=F32)
    parts = [taken[:, s * HALF : (s + 1) * HALF].reshape(shots, RD, HALF) for s in range(4)]
    slots_ref[...] = jnp.concatenate(parts, axis=1).astype(BF16)


def prepare(weight_first, weight_middle, weight_last, own):
    shapes = (
        (OUTER * 2 * CH, UNIT),
        (2 * CH, 3 * UNIT),
        (4 * RD, INNER * 2 * CH),
        (NT, 4 * HALF),
        (own.shape[0], 4 * RD, HALF),
    )
    return pl.pallas_call(
        prepare_body,
        out_shape=tuple(jax.ShapeDtypeStruct(s, BF16) for s in shapes),
        scratch_shapes=[pltpu.VMEM(shapes[2], F32)],
        compiler_params=pltpu.CompilerParams(vmem_limit_bytes=24 << 20),
        name="prepare",
    )(weight_first, weight_middle, weight_last, own)


def product(accs, lhs, rhs, use):
    rows, depth = lhs.shape
    for n in range(rhs.shape[1] // UNIT):
        held = accs[n % UNITS]
        for k in range(depth // UNIT):
            piece = rhs[k * UNIT : (k + 1) * UNIT, n * UNIT : (n + 1) * UNIT]
            pltpu.matmul_push_rhs(piece, k % 2, n % UNITS)
            for c in range(rows // BLK):
                piece = lhs[c * BLK : (c + 1) * BLK, k * UNIT : (k + 1) * UNIT]
                pltpu.matmul_acc_lhs(held[c], piece, load_staged_rhs=k % 2 if c == 0 else None)
        for c in range(rows // BLK):
            use(n, c, pltpu.matmul_pop(held[c]))


def run(jobs):
    def push(number):
        for unit in range(UNITS):
            pltpu.matmul_push_rhs(jobs[number][0](unit), number % 2, unit)

    push(0)
    for number, (_, products, after) in enumerate(jobs):
        if number + 1 < len(jobs):
            push(number + 1)
        for n, (acc, lhs) in enumerate(products):
            for unit in range(UNITS):
                staged = number % 2 if n == 0 else None
                pltpu.matmul_acc_lhs(acc(unit), lhs(), load_staged_rhs=staged)
        for act in after:
            act()


def denoise_loop(
    offset_ref, target_ref, near_ref, far_ref, own, first_ref, middle_ref, last_ref, split_ref,
    denoised_ref, sent_ref, near, far, h1_even, h1_odd, h2_even, h2_odd, cleaned, rows4, accs,
):
    shots = own.shape[0]
    pairs = shots // UNITS
    per_block = BLK // RD

    for ref, held in ((near_ref, near), (far_ref, far)):
        def put(slot, c, part, held=held):
            for row in range(4):
                at = pl.ds(slot * 4 + row, shots, stride=SIDE)
                for half in range(HALF // LANES):
                    lanes = slice(half * LANES, (half + 1) * LANES)
                    held[half, at, :] = part[row * shots : (row + 1) * shots, lanes]

        edge = ref[...].reshape(EDGE * shots, NT)
        rest = jnp.zeros((BLK - EDGE * shots, NT), BF16)
        product(accs, jnp.concatenate([edge, rest], axis=0), split_ref, put)

    def taps(pair):
        def right(unit):
            shot = pair * UNITS + unit
            rows = pl.ds(pl.multiple_of(shot * SIDE, SIDE), SIDE)
            rest = jnp.zeros((UNIT - 4 * RD - 2 * SIDE, HALF), BF16)
            sides = [
                jnp.concatenate([side[0, rows, :], side[1, rows, :]], axis=1).astype(BF16)
                for side in (near, far)
            ]
            return jnp.concatenate([sides[0], own[shot], sides[1], rest], axis=0)

        return right

    def first_done(h1, receiver):
        def act():
            for unit in range(UNITS):
                both = jnp.maximum(pltpu.matmul_pop(accs[unit][receiver % 3]), 0.0).astype(BF16)
                h1[unit, receiver, CH : 3 * CH, :] = both
                h1[unit, receiver, :CH, :] = delayed(both[CH:])
                h1[unit, receiver, 3 * CH :, :] = advanced(both[:CH])

        return act

    def middle_done(h2, receiver):
        def act():
            for unit in range(UNITS):
                both = jnp.maximum(pltpu.matmul_pop(accs[unit][3 + receiver % 4]), 0.0)
                h2[unit, receiver * 2 * CH : (receiver + 1) * 2 * CH, :] = both.astype(BF16)

        return act

    def last_done(pair):
        def act():
            for unit in range(UNITS):
                shot = pair * UNITS + unit
                parts = pltpu.matmul_pop(accs[unit][7])
                seen = own[shot].astype(F32)
                rows = pl.ds(pl.multiple_of(shot * RD, RD), RD)
                even = parts[:RD] + delayed(parts[2 * RD : 3 * RD])
                odd = parts[RD : 2 * RD] + advanced(parts[3 * RD :])
                cleaned[rows, :HALF] = seen[RD : 2 * RD] - even
                cleaned[rows, HALF:] = seen[2 * RD : 3 * RD] - odd

        return act

    def first_job(pair, receivers):
        products = [
            (
                lambda unit, r=r: accs[unit][r % 3],
                lambda r=r: first_ref[r * 2 * CH : (r + 1) * 2 * CH, :],
            )
            for r in receivers
        ]
        return taps(pair), products, []

    def middle_job(h1, receiver):
        products = [
            (
                lambda unit, r=receiver - across: accs[unit][3 + r % 4],
                lambda across=across: middle_ref[:, across * UNIT : (across + 1) * UNIT],
            )
            for across in (2, 1, 0)
            if 0 <= receiver - across < INNER
        ]
        return lambda unit: h1[unit, receiver], products, []

    def last_job(h2, number):
        lanes = slice(number * UNIT, (number + 1) * UNIT)
        products = [(lambda unit: accs[unit][7], lambda: last_ref[:, lanes])]
        return lambda unit: h2[unit, lanes, :], products, []

    def stage(now, later, before):
        jobs = []
        for r in range(OUTER):
            if later and r % 3 == 0:
                jobs.append(first_job(later[0], range(r, r + 3)))
            if now:
                jobs.append(middle_job(now[0], r))
            if later:
                jobs[-1][2].append(first_done(later[1], r))
            if now and r >= 3:
                jobs[-1][2].append(middle_done(now[1], r - 3))
            if before and r % 2 == 1 and r < INNER:
                jobs.append(last_job(before[1], r // 2))
            if before and r == INNER:
                jobs[-1][2].append(last_done(before[0]))
        return jobs, [middle_done(now[1], INNER - 1)] if now else []

    def chain(*stages):
        jobs, tail = [], []
        for more, end in stages:
            more[0][2].extend(tail)
            jobs, tail = jobs + more, end
        jobs[-1][2].extend(tail)
        run(jobs)

    buffers = ((h1_even, h2_even), (h1_odd, h2_odd))

    def full(pair, parity):
        now, other = buffers[parity], buffers[1 - parity]
        return stage(now, (pair + 1, other[0]), (pair - 1, other[1]))

    def several(step, carry):
        pair = STAGES * step + 1
        chain(*[full(pair + n, (n + 1) % 2) for n in range(STAGES)])
        return carry

    chain(stage(None, (0, h1_even), None), stage(buffers[0], (1, h1_odd), None))
    steps = (pairs - 2) // STAGES
    lax.fori_loop(0, steps, several, 0)
    rest = [full(pair, pair % 2) for pair in range(STAGES * steps + 1, pairs - 1)]
    end = [last_job(h2_odd, n) for n in range(INNER // 2)], [last_done(pairs - 1)]
    chain(*rest, stage(buffers[1], None, (pairs - 2, h2_even)), end)

    lane = lax.broadcasted_iota(jnp.int32, (NT, NT), 0)
    time = lax.broadcasted_iota(jnp.int32, (NT, NT), 1)
    merge = one_hot(time == 2 * (lane % HALF) + lane // HALF)
    owners = sent_ref.shape[0]
    kept = BLK // owners

    def put(n, c, part):
        lanes = slice(n * UNIT, (n + 1) * UNIT)
        shot = slice(c * per_block, (c + 1) * per_block)
        denoised_ref[shot, :, lanes] = part.astype(BF16).reshape(per_block, RD, UNIT)
        rows4[:, c * kept : (c + 1) * kept, lanes] = part.reshape(owners, kept, UNIT)

    product(accs, cleaned[...].astype(BF16), merge, put)
    sent_ref[:, :, :NT] = rows4[...].astype(BF16)
    shape = (sent_ref.shape[1], LANES)
    block = lax.broadcasted_iota(jnp.int32, shape, 0) // kept
    first_half = lax.broadcasted_iota(jnp.int32, shape, 1) < LANES // 2
    tag = jnp.zeros(shape, jnp.int32)
    for c in range(shots * RD // BLK):
        tag = jnp.where(block == c, jnp.where(first_half, target_ref[c], offset_ref[c]), tag)
    tag = tag.astype(F32).astype(BF16)
    sent_ref[:, :, NT:] = jnp.broadcast_to(tag[None], (owners, *shape))


def denoise_body(*refs):
    pl.run_scoped(
        lambda *accs: denoise_loop(*refs, (accs[:8], accs[8:])),
        *[
            pltpu.ACC(unit)((BLK if number < 7 else 4 * RD, UNIT), F32)
            for unit in range(UNITS)
            for number in range(8)
        ],
    )


def denoise(offsets, targets, near, far, slots, first, middle, last, split):
    shots, blocks = slots.shape[0], offsets.shape[0]
    owners = lax.axis_size("tile")
    sent = (owners, blocks * BLK // owners, NT + LANES)
    scalars = pl.BlockSpec(memory_space=pltpu.SMEM)
    whole = pl.BlockSpec(memory_space=pltpu.VMEM)
    macs = shots * RD * NT * CH * (9 * CH + 18)
    return pl.pallas_call(
        denoise_body,
        out_shape=(jax.ShapeDtypeStruct((shots, RD, NT), BF16), jax.ShapeDtypeStruct(sent, BF16)),
        in_specs=[scalars] * 2 + [whole] * 7,
        out_specs=(whole, whole),
        scratch_shapes=[pltpu.VMEM((HALF // LANES, shots * SIDE, LANES), F32)] * 2
        + [pltpu.VMEM((UNITS, OUTER, UNIT, HALF), BF16)] * 2
        + [pltpu.VMEM((UNITS, INNER * 2 * CH, HALF), BF16)] * 2
        + [pltpu.VMEM((shots * RD, NT), F32), pltpu.VMEM((*sent[:2], NT), F32)],
        compiler_params=pltpu.CompilerParams(vmem_limit_bytes=40 << 20),
        cost_estimate=pl.CostEstimate(flops=2 * macs, transcendentals=0, bytes_accessed=4 << 20),
        name="denoise",
    )(offsets, targets, near, far, slots, first, middle, last, split)


def stack_body(came_ref, map_ref, *part_refs):
    tiles, kept, _ = came_ref.shape
    rows = kept * BLK // (SH * RD)
    count = tiles * kept
    came = came_ref[...].reshape(count, NT + LANES)
    target = came[:, NT : NT + 1].astype(F32).astype(jnp.int32)
    offset = came[:, NT + LANES // 2 : NT + LANES // 2 + 1].astype(F32)
    traces = came[:, :NT]
    none = jnp.zeros_like(traces)
    wide = [jnp.where(offset == o, traces, none) for o in range(OB)]
    corrected = jnp.dot(
        jnp.concatenate(wide, axis=1), map_ref[...], preferred_element_type=F32
    )
    groups = len(part_refs)
    owned = MBLK // groups
    place = ((target // owned) ^ lax.axis_index("grp")) * owned + target % owned
    row = lax.broadcasted_iota(jnp.int32, (count, MBLK * rows), 0) % rows
    column = lax.broadcasted_iota(jnp.int32, (count, MBLK * rows), 1)
    chosen = one_hot((place == column // rows) & (row == column % rows))
    total = None
    for _ in range(3):
        part = corrected.astype(BF16)
        corrected = corrected - part.astype(F32)
        term = lax.dot_general(chosen, part, (((0,), (0,)), ((), ())), preferred_element_type=F32)
        total = term if total is None else total + term
    for number, ref in enumerate(part_refs):
        part = total[number * owned * rows : (number + 1) * owned * rows]
        ref[...] = part.reshape(ref.shape)


def stack(came, moveout_maps, groups):
    rows = came.shape[1] * BLK // (SH * RD)
    part = jax.ShapeDtypeStruct((MBLK // groups, rows, NT), F32)
    return pl.pallas_call(
        stack_body,
        out_shape=(part,) * groups,
        compiler_params=pltpu.CompilerParams(vmem_limit_bytes=40 << 20),
        name="stack",
    )(came, moveout_maps.reshape(OB * NT, NT))


def edges(own):
    odd = lax.axis_index("tile") % 2 == 1
    start, end = own[:, :EDGE, :].transpose(1, 0, 2), own[:, -EDGE:, :].transpose(1, 0, 2)
    return jnp.where(odd, start, end), jnp.where(odd, end, start)


def on_device(
    shot_data, weight_first, weight_middle, weight_last, moveout_maps, block_offset, block_target
):
    tiles, groups = lax.axis_size("tile"), lax.axis_size("grp")
    (own, weight_first, weight_middle, weight_last, block_offset, block_target) = (
        pltpu.with_memory_space_constraint(a, pltpu.HBM)
        for a in (
            shot_data,
            weight_first,
            weight_middle.reshape(9 * CH, CH),
            weight_last,
            block_offset,
            block_target.reshape(-1),
        )
    )
    near, far = edges(shot_data)
    near = lax.ppermute(near, "tile", [(i, i ^ 1) for i in range(tiles)])
    pairs = [(i, i + 1) for i in range(1, tiles - 1, 2)]
    far = lax.ppermute(far, "tile", pairs + [(j, i) for i, j in pairs])
    *weights, split, slots = prepare(weight_first, weight_middle, weight_last, own)
    denoised, sent = denoise(block_offset, block_target, near, far, slots, *weights, split)
    came = lax.all_to_all(sent, "tile", 0, 0, tiled=True)
    stacked, *parts = stack(came, moveout_maps, groups)
    for apart in (2, 1, 3):
        part = lax.ppermute(parts[apart - 1], "grp", [(g, g ^ apart) for g in range(groups)])
        stacked = stacked + part
    return denoised, stacked


def solution(mesh):
    in_specs = (
        P("grp", "tile", None),
        P(),
        P(),
        P(),
        P(),
        P(("grp", "tile")),
        P(("grp", "tile"), None),
    )
    out_specs = (P("grp", "tile", None), P("grp", "tile", None))
    return jax.shard_map(
        on_device, mesh=mesh, in_specs=in_specs, out_specs=out_specs, check_vma=False
    )
```

```python
import jax
import jax.numpy as jnp
from jax import lax
from jax.experimental import pallas as pl
from jax.experimental.pallas import tpu as pltpu
from jax.sharding import PartitionSpec as P

CH = 64
RD = 8
SH = 32
NT = 512
OB = 8
BLK = 128
MBLK = 32
LANES = 128
UNIT = 256
UNITS = 2
HALF = NT // 2
OUTER = RD + 4
INNER = RD + 2
EDGE = 3
SIDE = 16
STAGES = 4
F32 = jnp.float32
BF16 = jnp.bfloat16


def at_lane(shape, lane):
    return lax.broadcasted_iota(jnp.int32, shape, 1) % HALF == lane


def delayed(rows):
    return jnp.where(at_lane(rows.shape, 0), jnp.zeros_like(rows), pltpu.roll(rows, 1, 1))


def advanced(rows):
    last = rows.shape[1] - 1
    return jnp.where(at_lane(rows.shape, HALF - 1), jnp.zeros_like(rows), pltpu.roll(rows, last, 1))


def one_hot(condition):
    return condition.astype(F32).astype(BF16)


def prepare_body(tap1_ref, tap2_ref, tap3_ref, own_ref, first_ref, middle_ref, last_ref, split_ref, slots_ref, wide):
    tile = lax.axis_index("tile")
    low = (tile > 0).astype(F32)
    high = (tile < lax.axis_size("tile") - 1).astype(F32)

    shape = (9, UNIT)
    tap = lax.broadcasted_iota(jnp.int32, shape, 0)
    column = lax.broadcasted_iota(jnp.int32, shape, 1)
    inner = column - SIDE
    outer = inner - 4 * RD
    is_near, is_own = column < SIDE, inner < 4 * RD
    odd = tile % 2
    near, far = (EDGE + RD) * (1 - odd), (EDGE + RD) * odd
    across = jnp.where(is_near, column % 4 + near, jnp.where(is_own, inner % RD + EDGE, outer % 4 + far))
    delay = jnp.where(is_near, column // 4, jnp.where(is_own, inner // RD, outer // 4))
    used = (column < 2 * SIDE + 4 * RD) & ((is_near | (inner >= 4 * RD)) & (column % 4 < EDGE) | (inner >= 0) & is_own)
    for receiver in range(OUTER):
        inside = low if receiver < 2 else high if receiver >= OUTER - 2 else None
        for phase in range(2):
            a, d = across - receiver, delay - phase
            place = (tap == 3 * a + d) & (a >= 0) & (a <= 2) & (d >= 0) & (d <= 2) & used
            place = place.astype(F32)
            if inside is not None:
                place = place * inside
            block = lax.dot_general(
                tap1_ref[...], place.astype(BF16), (((0,), (0,)), ((), ())), preferred_element_type=F32
            )
            row = (2 * receiver + phase) * CH
            first_ref[row : row + CH, :] = block.astype(BF16)

    none = jnp.zeros((CH, CH), BF16)
    for across in range(3):
        taps = [tap2_ref[(3 * across + d) * CH : (3 * across + d + 1) * CH, :] for d in range(3)]
        lanes = slice(across * UNIT, (across + 1) * UNIT)
        middle_ref[:CH, lanes] = jnp.concatenate([*taps, none], axis=1)
        middle_ref[CH:, lanes] = jnp.concatenate([none, *taps], axis=1)

    none = jnp.zeros((1, CH), F32)
    taps = [tap3_ref[k : k + 1, :].astype(F32) for k in range(9)]
    kinds = [
        [taps[3 * a + 1] for a in range(3)], [taps[3 * a + 2] for a in range(3)],
        [taps[3 * a] for a in range(3)], [taps[3 * a + 1] for a in range(3)],
        [none] * 3, [taps[3 * a] for a in range(3)],
        [taps[3 * a + 2] for a in range(3)], [none] * 3,
    ]
    wide[...] = jnp.zeros_like(wide)
    for kind in range(4):
        row = [t for pair in zip(kinds[2 * kind], kinds[2 * kind + 1]) for t in pair]
        row = jnp.concatenate(row, axis=1)
        for receiver in range(RD):
            at = kind * RD + receiver
            wide[at : at + 1, receiver * 2 * CH : (receiver + 3) * 2 * CH] = row
    wide[:, : 2 * CH] = wide[:, : 2 * CH] * low
    wide[:, (INNER - 1) * 2 * CH :] = wide[:, (INNER - 1) * 2 * CH :] * high
    last_ref[...] = wide[...].astype(BF16)

    time = lax.broadcasted_iota(jnp.int32, (NT, 4 * HALF), 0)
    lane = lax.broadcasted_iota(jnp.int32, (NT, 4 * HALF), 1)
    split = one_hot(time == 2 * (lane % HALF) + lane // HALF - 1)
    split_ref[...] = split
    shots = own_ref.shape[0]
    taken = jnp.dot(own_ref[...].reshape(shots * RD, NT), split, preferred_element_type=F32)
    parts = [taken[:, s * HALF : (s + 1) * HALF].reshape(shots, RD, HALF) for s in range(4)]
    slots_ref[...] = jnp.concatenate(parts, axis=1).astype(BF16)


def prepare(weight_first, weight_middle, weight_last, own):
    shapes = (
        (OUTER * 2 * CH, UNIT),
        (2 * CH, 3 * UNIT),
        (4 * RD, INNER * 2 * CH),
        (NT, 4 * HALF),
        (own.shape[0], 4 * RD, HALF),
    )
    return pl.pallas_call(
        prepare_body,
        out_shape=tuple(jax.ShapeDtypeStruct(s, BF16) for s in shapes),
        scratch_shapes=[pltpu.VMEM(shapes[2], F32)],
        compiler_params=pltpu.CompilerParams(vmem_limit_bytes=24 << 20),
        name="prepare",
    )(weight_first, weight_middle, weight_last, own)


def products(accs, items):
    taken = [0] * UNITS
    done = []
    for lhs, rhs, use in items:
        rows, depth = lhs.shape
        for n in range(rhs.shape[1] // UNIT):
            unit = n % UNITS
            held = accs[unit][taken[unit] : taken[unit] + rows // BLK]
            taken[unit] += len(held)
            for k in range(depth // UNIT):
                piece = rhs[k * UNIT : (k + 1) * UNIT, n * UNIT : (n + 1) * UNIT]
                pltpu.matmul_push_rhs(piece, k % 2, unit)
                for c, acc in enumerate(held):
                    piece = lhs[c * BLK : (c + 1) * BLK, k * UNIT : (k + 1) * UNIT]
                    pltpu.matmul_acc_lhs(acc, piece, load_staged_rhs=k % 2 if c == 0 else None)
            done += [(use, n, c, acc) for c, acc in enumerate(held)]
    for use, n, c, acc in done:
        use(n, c, pltpu.matmul_pop(acc))


def run(jobs):
    def push(number):
        for unit in range(UNITS):
            pltpu.matmul_push_rhs(jobs[number][0](unit), number % 2, unit)

    push(0)
    for number, (_, products, after) in enumerate(jobs):
        if number + 1 < len(jobs):
            push(number + 1)
        for n, (acc, lhs) in enumerate(products):
            for unit in range(UNITS):
                staged = number % 2 if n == 0 else None
                pltpu.matmul_acc_lhs(acc(unit), lhs(), load_staged_rhs=staged)
        for act in after:
            act()


def denoise_loop(
    offset_ref, target_ref, near_ref, far_ref, own, first_ref, middle_ref, last_ref, split_ref,
    denoised_ref, sent_ref, near, far, h1_even, h1_odd, h2_even, h2_odd, cleaned, rows4, accs,
):
    shots = own.shape[0]
    pairs = shots // UNITS
    per_block = BLK // RD

    items = []
    for ref, held in ((near_ref, near), (far_ref, far)):
        def keep(slot, c, part, held=held):
            for row in range(4):
                at = pl.ds(slot * 4 + row, shots, stride=SIDE)
                for half in range(HALF // LANES):
                    lanes = slice(half * LANES, (half + 1) * LANES)
                    held[half, at, :] = part[row * shots : (row + 1) * shots, lanes]

        edge = ref[...].reshape(EDGE * shots, NT)
        rest = jnp.zeros((BLK - EDGE * shots, NT), BF16)
        items.append((jnp.concatenate([edge, rest], axis=0), split_ref, keep))
    products(accs, items)

    def taps(pair):
        def right(unit):
            shot = pair * UNITS + unit
            rows = pl.ds(pl.multiple_of(shot * SIDE, SIDE), SIDE)
            rest = jnp.zeros((UNIT - 4 * RD - 2 * SIDE, HALF), BF16)
            sides = [
                jnp.concatenate([side[0, rows, :], side[1, rows, :]], axis=1).astype(BF16)
                for side in (near, far)
            ]
            return jnp.concatenate([sides[0], own[shot], sides[1], rest], axis=0)

        return right

    def first_done(h1, receiver):
        def act():
            for unit in range(UNITS):
                both = jnp.maximum(pltpu.matmul_pop(accs[unit][receiver % 3]), 0.0).astype(BF16)
                h1[unit, receiver, CH : 3 * CH, :] = both
                h1[unit, receiver, :CH, :] = delayed(both[CH:])
                h1[unit, receiver, 3 * CH :, :] = advanced(both[:CH])

        return act

    def middle_done(h2, receiver):
        def act():
            for unit in range(UNITS):
                both = jnp.maximum(pltpu.matmul_pop(accs[unit][3 + receiver % 4]), 0.0)
                h2[unit, receiver * 2 * CH : (receiver + 1) * 2 * CH, :] = both.astype(BF16)

        return act

    def last_done(pair):
        def act():
            for unit in range(UNITS):
                shot = pair * UNITS + unit
                parts = pltpu.matmul_pop(accs[unit][7])
                seen = own[shot].astype(F32)
                rows = pl.ds(pl.multiple_of(shot * RD, RD), RD)
                even = parts[:RD] + delayed(parts[2 * RD : 3 * RD])
                odd = parts[RD : 2 * RD] + advanced(parts[3 * RD :])
                cleaned[rows, :HALF] = seen[RD : 2 * RD] - even
                cleaned[rows, HALF:] = seen[2 * RD : 3 * RD] - odd

        return act

    def first_job(pair, receivers):
        products = [
            (
                lambda unit, r=r: accs[unit][r % 3],
                lambda r=r: first_ref[r * 2 * CH : (r + 1) * 2 * CH, :],
            )
            for r in receivers
        ]
        return taps(pair), products, []

    def middle_job(h1, receiver):
        products = [
            (
                lambda unit, r=receiver - across: accs[unit][3 + r % 4],
                lambda across=across: middle_ref[:, across * UNIT : (across + 1) * UNIT],
            )
            for across in (2, 1, 0)
            if 0 <= receiver - across < INNER
        ]
        return lambda unit: h1[unit, receiver], products, []

    def last_job(h2, number):
        lanes = slice(number * UNIT, (number + 1) * UNIT)
        products = [(lambda unit: accs[unit][7], lambda: last_ref[:, lanes])]
        return lambda unit: h2[unit, lanes, :], products, []

    def stage(now, later, before):
        jobs = []
        for r in range(OUTER):
            if later and r % 3 == 0:
                jobs.append(first_job(later[0], range(r, r + 3)))
            if now:
                jobs.append(middle_job(now[0], r))
            if later:
                jobs[-1][2].append(first_done(later[1], r))
            if now and r >= 3:
                jobs[-1][2].append(middle_done(now[1], r - 3))
            if before and r % 2 == 1 and r < INNER:
                jobs.append(last_job(before[1], r // 2))
            if before and r == INNER:
                jobs[-1][2].append(last_done(before[0]))
        return jobs, [middle_done(now[1], INNER - 1)] if now else []

    def chain(*stages):
        jobs, tail = [], []
        for more, end in stages:
            more[0][2].extend(tail)
            jobs, tail = jobs + more, end
        jobs[-1][2].extend(tail)
        run(jobs)

    buffers = ((h1_even, h2_even), (h1_odd, h2_odd))

    def full(pair, parity):
        now, other = buffers[parity], buffers[1 - parity]
        return stage(now, (pair + 1, other[0]), (pair - 1, other[1]))

    def several(step, carry):
        pair = STAGES * step + 1
        chain(*[full(pair + n, (n + 1) % 2) for n in range(STAGES)])
        return carry

    chain(stage(None, (0, h1_even), None), stage(buffers[0], (1, h1_odd), None))
    steps = (pairs - 2) // STAGES
    lax.fori_loop(0, steps, several, 0)
    rest = [full(pair, pair % 2) for pair in range(STAGES * steps + 1, pairs - 1)]
    end = [last_job(h2_odd, n) for n in range(INNER // 2)], [last_done(pairs - 1)]
    chain(*rest, stage(buffers[1], None, (pairs - 2, h2_even)), end)

    lane = lax.broadcasted_iota(jnp.int32, (NT, NT), 0)
    time = lax.broadcasted_iota(jnp.int32, (NT, NT), 1)
    merge = one_hot(time == 2 * (lane % HALF) + lane // HALF)
    owners = sent_ref.shape[0]
    kept = BLK // owners

    def put(n, c, part):
        lanes = slice(n * UNIT, (n + 1) * UNIT)
        shot = slice(c * per_block, (c + 1) * per_block)
        denoised_ref[shot, :, lanes] = part.astype(BF16).reshape(per_block, RD, UNIT)
        rows4[:, c * kept : (c + 1) * kept, lanes] = part.reshape(owners, kept, UNIT)

    products(accs, [(cleaned[...].astype(BF16), merge, put)])
    sent_ref[:, :, :NT] = rows4[...].astype(BF16)
    shape = (sent_ref.shape[1], LANES)
    block = lax.broadcasted_iota(jnp.int32, shape, 0) // kept
    first_half = lax.broadcasted_iota(jnp.int32, shape, 1) < LANES // 2
    tag = jnp.zeros(shape, jnp.int32)
    for c in range(shots * RD // BLK):
        tag = jnp.where(block == c, jnp.where(first_half, target_ref[c], offset_ref[c]), tag)
    tag = tag.astype(F32).astype(BF16)
    sent_ref[:, :, NT:] = jnp.broadcast_to(tag[None], (owners, *shape))


def denoise_body(*refs):
    pl.run_scoped(
        lambda *accs: denoise_loop(*refs, (accs[:8], accs[8:])),
        *[
            pltpu.ACC(unit)((BLK if number < 7 else 4 * RD, UNIT), F32)
            for unit in range(UNITS)
            for number in range(8)
        ],
    )


def denoise(offsets, targets, near, far, slots, first, middle, last, split):
    shots, blocks = slots.shape[0], offsets.shape[0]
    owners = lax.axis_size("tile")
    sent = (owners, blocks * BLK // owners, NT + LANES)
    scalars = pl.BlockSpec(memory_space=pltpu.SMEM)
    whole = pl.BlockSpec(memory_space=pltpu.VMEM)
    macs = shots * RD * NT * CH * (9 * CH + 18)
    return pl.pallas_call(
        denoise_body,
        out_shape=(pltpu.VMEM((shots, RD, NT), BF16), jax.ShapeDtypeStruct(sent, BF16)),
        in_specs=[scalars] * 2 + [whole] * 7,
        out_specs=(whole, whole),
        scratch_shapes=[pltpu.VMEM((HALF // LANES, shots * SIDE, LANES), F32)] * 2
        + [pltpu.VMEM((UNITS, OUTER, UNIT, HALF), BF16)] * 2
        + [pltpu.VMEM((UNITS, INNER * 2 * CH, HALF), BF16)] * 2
        + [pltpu.VMEM((shots * RD, NT), F32), pltpu.VMEM((*sent[:2], NT), F32)],
        compiler_params=pltpu.CompilerParams(vmem_limit_bytes=40 << 20),
        cost_estimate=pl.CostEstimate(flops=2 * macs, transcendentals=0, bytes_accessed=4 << 20),
        name="denoise",
    )(offsets, targets, near, far, slots, first, middle, last, split)


def stack_body(came_ref, map_ref, *part_refs):
    tiles, kept, _ = came_ref.shape
    rows = kept * BLK // (SH * RD)
    count = tiles * kept
    came = came_ref[...].reshape(count, NT + LANES)
    target = came[:, NT : NT + 1].astype(F32).astype(jnp.int32)
    offset = came[:, NT + LANES // 2 : NT + LANES // 2 + 1].astype(F32)
    traces = came[:, :NT]
    none = jnp.zeros_like(traces)
    wide = [jnp.where(offset == o, traces, none) for o in range(OB)]
    corrected = jnp.dot(
        jnp.concatenate(wide, axis=1), map_ref[...], preferred_element_type=F32
    )
    groups = len(part_refs)
    owned = MBLK // groups
    place = ((target // owned) ^ lax.axis_index("grp")) * owned + target % owned
    row = lax.broadcasted_iota(jnp.int32, (count, MBLK * rows), 0) % rows
    column = lax.broadcasted_iota(jnp.int32, (count, MBLK * rows), 1)
    chosen = one_hot((place == column // rows) & (row == column % rows))
    total = None
    for _ in range(3):
        part = corrected.astype(BF16)
        corrected = corrected - part.astype(F32)
        term = lax.dot_general(chosen, part, (((0,), (0,)), ((), ())), preferred_element_type=F32)
        total = term if total is None else total + term
    for number, ref in enumerate(part_refs):
        part = total[number * owned * rows : (number + 1) * owned * rows]
        ref[...] = part.reshape(ref.shape)


def stack(came, moveout_maps, groups):
    rows = came.shape[1] * BLK // (SH * RD)
    part = jax.ShapeDtypeStruct((MBLK // groups, rows, NT), F32)
    return pl.pallas_call(
        stack_body,
        out_shape=(part,) * groups,
        compiler_params=pltpu.CompilerParams(vmem_limit_bytes=40 << 20),
        name="stack",
    )(came, moveout_maps.reshape(OB * NT, NT))


def edges(own):
    odd = lax.axis_index("tile") % 2 == 1
    start, end = own[:, :EDGE, :].transpose(1, 0, 2), own[:, -EDGE:, :].transpose(1, 0, 2)
    return jnp.where(odd, start, end), jnp.where(odd, end, start)


def on_device(
    shot_data, weight_first, weight_middle, weight_last, moveout_maps, block_offset, block_target
):
    tiles, groups = lax.axis_size("tile"), lax.axis_size("grp")
    (own, weight_first, weight_middle, weight_last, block_offset, block_target) = (
        pltpu.with_memory_space_constraint(a, pltpu.HBM)
        for a in (
            shot_data,
            weight_first,
            weight_middle.reshape(9 * CH, CH),
            weight_last,
            block_offset,
            block_target.reshape(-1),
        )
    )
    near, far = edges(shot_data)
    near = lax.ppermute(near, "tile", [(i, i ^ 1) for i in range(tiles)])
    pairs = [(i, i + 1) for i in range(1, tiles - 1, 2)]
    far = lax.ppermute(far, "tile", pairs + [(j, i) for i, j in pairs])
    *weights, split, slots = prepare(weight_first, weight_middle, weight_last, own)
    denoised, sent = denoise(block_offset, block_target, near, far, slots, *weights, split)
    came = lax.all_to_all(sent, "tile", 0, 0, tiled=True)
    stacked, *parts = stack(came, moveout_maps, groups)
    for apart in (2, 1, 3):
        part = lax.ppermute(parts[apart - 1], "grp", [(g, g ^ apart) for g in range(groups)])
        stacked = stacked + part
    return denoised, stacked


def solution(mesh):
    in_specs = (
        P("grp", "tile", None),
        P(),
        P(),
        P(),
        P(),
        P(("grp", "tile")),
        P(("grp", "tile"), None),
    )
    out_specs = (P("grp", "tile", None), P("grp", "tile", None))
    return jax.shard_map(
        on_device, mesh=mesh, in_specs=in_specs, out_specs=out_specs, check_vma=False
    )
```

```python
import jax
import jax.numpy as jnp
from jax import lax
from jax.experimental import pallas as pl
from jax.experimental.pallas import tpu as pltpu
from jax.sharding import PartitionSpec as P

CH = 64
RD = 8
SH = 32
NT = 512
OB = 8
BLK = 128
MBLK = 32
LANES = 128
UNIT = 256
UNITS = 2
HALF = NT // 2
OUTER = RD + 4
INNER = RD + 2
EDGE = 3
SIDE = 16
STAGES = 4
F32 = jnp.float32
BF16 = jnp.bfloat16


def at_lane(shape, lane):
    return lax.broadcasted_iota(jnp.int32, shape, 1) % HALF == lane


def delayed(rows):
    return jnp.where(at_lane(rows.shape, 0), jnp.zeros_like(rows), pltpu.roll(rows, 1, 1))


def advanced(rows):
    last = rows.shape[1] - 1
    return jnp.where(at_lane(rows.shape, HALF - 1), jnp.zeros_like(rows), pltpu.roll(rows, last, 1))


def one_hot(condition):
    return condition.astype(F32).astype(BF16)


def prepare_body(tap1_ref, tap2_ref, tap3_ref, own_ref, first_ref, middle_ref, last_ref, split_ref, slots_ref, wide):
    tile = lax.axis_index("tile")
    low = (tile > 0).astype(F32)
    high = (tile < lax.axis_size("tile") - 1).astype(F32)

    shape = (9, UNIT)
    tap = lax.broadcasted_iota(jnp.int32, shape, 0)
    column = lax.broadcasted_iota(jnp.int32, shape, 1)
    inner = column - SIDE
    outer = inner - 4 * RD
    is_near, is_own = column < SIDE, inner < 4 * RD
    odd = tile % 2
    near, far = (EDGE + RD) * (1 - odd), (EDGE + RD) * odd
    across = jnp.where(is_near, column % 4 + near, jnp.where(is_own, inner % RD + EDGE, outer % 4 + far))
    delay = jnp.where(is_near, column // 4, jnp.where(is_own, inner // RD, outer // 4))
    used = (column < 2 * SIDE + 4 * RD) & ((is_near | (inner >= 4 * RD)) & (column % 4 < EDGE) | (inner >= 0) & is_own)
    for receiver in range(OUTER):
        inside = low if receiver < 2 else high if receiver >= OUTER - 2 else None
        for phase in range(2):
            a, d = across - receiver, delay - phase
            place = (tap == 3 * a + d) & (a >= 0) & (a <= 2) & (d >= 0) & (d <= 2) & used
            place = place.astype(F32)
            if inside is not None:
                place = place * inside
            block = lax.dot_general(
                tap1_ref[...], place.astype(BF16), (((0,), (0,)), ((), ())), preferred_element_type=F32
            )
            row = (2 * receiver + phase) * CH
            first_ref[row : row + CH, :] = block.astype(BF16)

    none = jnp.zeros((CH, CH), BF16)
    for across in range(3):
        taps = [tap2_ref[(3 * across + d) * CH : (3 * across + d + 1) * CH, :] for d in range(3)]
        lanes = slice(across * UNIT, (across + 1) * UNIT)
        middle_ref[:CH, lanes] = jnp.concatenate([*taps, none], axis=1)
        middle_ref[CH:, lanes] = jnp.concatenate([none, *taps], axis=1)

    none = jnp.zeros((1, CH), F32)
    taps = [tap3_ref[k : k + 1, :].astype(F32) for k in range(9)]
    kinds = [
        [taps[3 * a + 1] for a in range(3)], [taps[3 * a + 2] for a in range(3)],
        [taps[3 * a] for a in range(3)], [taps[3 * a + 1] for a in range(3)],
        [none] * 3, [taps[3 * a] for a in range(3)],
        [taps[3 * a + 2] for a in range(3)], [none] * 3,
    ]
    wide[...] = jnp.zeros_like(wide)
    for kind in range(4):
        row = [t for pair in zip(kinds[2 * kind], kinds[2 * kind + 1]) for t in pair]
        row = jnp.concatenate(row, axis=1)
        for receiver in range(RD):
            at = RD + receiver // 2 * RD + 2 * kind + receiver % 2
            wide[at : at + 1, receiver * 2 * CH : (receiver + 3) * 2 * CH] = row
    wide[:, : 2 * CH] = wide[:, : 2 * CH] * low
    wide[:, (INNER - 1) * 2 * CH :] = wide[:, (INNER - 1) * 2 * CH :] * high
    for n in range(INNER // 2):
        rows = slice(2 * n * RD, 2 * (n + 1) * RD)
        last_ref[rows, :] = wide[n * RD : (n + 2) * RD, n * UNIT : (n + 1) * UNIT].astype(BF16)

    time = lax.broadcasted_iota(jnp.int32, (NT, 4 * HALF), 0)
    lane = lax.broadcasted_iota(jnp.int32, (NT, 4 * HALF), 1)
    split = one_hot(time == 2 * (lane % HALF) + lane // HALF - 1)
    split_ref[...] = split
    shots = own_ref.shape[0]
    taken = jnp.dot(own_ref[...].reshape(shots * RD, NT), split, preferred_element_type=F32)
    parts = [taken[:, s * HALF : (s + 1) * HALF].reshape(shots, RD, HALF) for s in range(4)]
    slots_ref[...] = jnp.concatenate(parts, axis=1).astype(BF16)


def prepare(weight_first, weight_middle, weight_last, own):
    shapes = (
        (OUTER * 2 * CH, UNIT),
        (2 * CH, 3 * UNIT),
        (INNER * RD, UNIT),
        (NT, 4 * HALF),
        (own.shape[0], 4 * RD, HALF),
    )
    return pl.pallas_call(
        prepare_body,
        out_shape=tuple(jax.ShapeDtypeStruct(s, BF16) for s in shapes),
        scratch_shapes=[pltpu.VMEM(((INNER // 2 + 1) * RD, INNER * 2 * CH), F32)],
        compiler_params=pltpu.CompilerParams(vmem_limit_bytes=24 << 20),
        name="prepare",
    )(weight_first, weight_middle, weight_last, own)


def products(accs, items):
    taken = [0] * UNITS
    done = []
    for lhs, rhs, use in items:
        rows, depth = lhs.shape
        for n in range(rhs.shape[1] // UNIT):
            unit = n % UNITS
            held = accs[unit][taken[unit] : taken[unit] + rows // BLK]
            taken[unit] += len(held)
            for k in range(depth // UNIT):
                piece = rhs[k * UNIT : (k + 1) * UNIT, n * UNIT : (n + 1) * UNIT]
                pltpu.matmul_push_rhs(piece, k % 2, unit)
                for c, acc in enumerate(held):
                    piece = lhs[c * BLK : (c + 1) * BLK, k * UNIT : (k + 1) * UNIT]
                    pltpu.matmul_acc_lhs(acc, piece, load_staged_rhs=k % 2 if c == 0 else None)
            done += [(use, n, c, acc) for c, acc in enumerate(held)]
    for use, n, c, acc in done:
        use(n, c, pltpu.matmul_pop(acc))


def run(jobs):
    def push(number):
        for unit in range(UNITS):
            pltpu.matmul_push_rhs(jobs[number][0](unit), number % 2, unit)

    push(0)
    for number, (_, products, after) in enumerate(jobs):
        if number + 1 < len(jobs):
            push(number + 1)
        for n, (acc, lhs) in enumerate(products):
            for unit in range(UNITS):
                staged = number % 2 if n == 0 else None
                pltpu.matmul_acc_lhs(acc(unit), lhs(), load_staged_rhs=staged)
        for act in after:
            act()


def denoise_loop(
    offset_ref, target_ref, near_ref, far_ref, own, first_ref, middle_ref, last_ref, split_ref,
    denoised_ref, sent_ref, near, far, h1_even, h1_odd, h2_even, h2_odd, cleaned, rows4, accs,
):
    shots = own.shape[0]
    pairs = shots // UNITS
    per_block = BLK // RD

    items = []
    for ref, held in ((near_ref, near), (far_ref, far)):
        def keep(slot, c, part, held=held):
            for row in range(4):
                at = pl.ds(slot * 4 + row, shots, stride=SIDE)
                for half in range(HALF // LANES):
                    lanes = slice(half * LANES, (half + 1) * LANES)
                    held[half, at, :] = part[row * shots : (row + 1) * shots, lanes]

        edge = ref[...].reshape(EDGE * shots, NT)
        rest = jnp.zeros((BLK - EDGE * shots, NT), BF16)
        items.append((jnp.concatenate([edge, rest], axis=0), split_ref, keep))
    products(accs, items)

    def taps(pair):
        def right(unit):
            shot = pair * UNITS + unit
            rows = pl.ds(pl.multiple_of(shot * SIDE, SIDE), SIDE)
            rest = jnp.zeros((UNIT - 4 * RD - 2 * SIDE, HALF), BF16)
            sides = [
                jnp.concatenate([side[0, rows, :], side[1, rows, :]], axis=1).astype(BF16)
                for side in (near, far)
            ]
            return jnp.concatenate([sides[0], own[shot], sides[1], rest], axis=0)

        return right

    def first_done(h1, receiver):
        def act():
            for unit in range(UNITS):
                both = jnp.maximum(pltpu.matmul_pop(accs[unit][receiver % 3]), 0.0).astype(BF16)
                h1[unit, receiver, CH : 3 * CH, :] = both
                h1[unit, receiver, :CH, :] = delayed(both[CH:])
                h1[unit, receiver, 3 * CH :, :] = advanced(both[:CH])

        return act

    def middle_done(h2, receiver):
        def act():
            for unit in range(UNITS):
                both = jnp.maximum(pltpu.matmul_pop(accs[unit][3 + receiver % 4]), 0.0)
                h2[unit, receiver * 2 * CH : (receiver + 1) * 2 * CH, :] = both.astype(BF16)

        return act

    def last_done(pair):
        def act():
            for unit in range(UNITS):
                shot = pair * UNITS + unit
                parts = [pltpu.matmul_pop(acc) for acc in accs[unit][7:]]
                sums = [low[RD:] + high[:RD] for low, high in zip(parts, parts[1:])]
                kinds = [jnp.concatenate([p[2 * k : 2 * k + 2] for p in sums], axis=0) for k in range(4)]
                seen = own[shot].astype(F32)
                rows = pl.ds(pl.multiple_of(shot * RD, RD), RD)
                even = kinds[0] + delayed(kinds[2])
                odd = kinds[1] + advanced(kinds[3])
                cleaned[rows, :HALF] = seen[RD : 2 * RD] - even
                cleaned[rows, HALF:] = seen[2 * RD : 3 * RD] - odd

        return act

    def first_job(pair, receivers):
        products = [
            (
                lambda unit, r=r: accs[unit][r % 3],
                lambda r=r: first_ref[r * 2 * CH : (r + 1) * 2 * CH, :],
            )
            for r in receivers
        ]
        return taps(pair), products, []

    def middle_job(h1, receiver):
        products = [
            (
                lambda unit, r=receiver - across: accs[unit][3 + r % 4],
                lambda across=across: middle_ref[:, across * UNIT : (across + 1) * UNIT],
            )
            for across in (2, 1, 0)
            if 0 <= receiver - across < INNER
        ]
        return lambda unit: h1[unit, receiver], products, []

    def last_job(h2, number):
        lanes = slice(number * UNIT, (number + 1) * UNIT)
        rows = slice(2 * number * RD, 2 * (number + 1) * RD)
        products = [(lambda unit: accs[unit][7 + number], lambda: last_ref[rows, :])]
        return lambda unit: h2[unit, lanes, :], products, []

    def stage(now, later, before):
        jobs = []
        for r in range(OUTER):
            if later and r % 3 == 0:
                jobs.append(first_job(later[0], range(r, r + 3)))
            if now:
                jobs.append(middle_job(now[0], r))
            if later:
                jobs[-1][2].append(first_done(later[1], r))
            if now and r >= 3:
                jobs[-1][2].append(middle_done(now[1], r - 3))
            if before and r % 2 == 1 and r < INNER:
                jobs.append(last_job(before[1], r // 2))
            if before and r == INNER:
                jobs[-1][2].append(last_done(before[0]))
        return jobs, [middle_done(now[1], INNER - 1)] if now else []

    def chain(*stages):
        jobs, tail = [], []
        for more, end in stages:
            more[0][2].extend(tail)
            jobs, tail = jobs + more, end
        jobs[-1][2].extend(tail)
        run(jobs)

    buffers = ((h1_even, h2_even), (h1_odd, h2_odd))

    def full(pair, parity):
        now, other = buffers[parity], buffers[1 - parity]
        return stage(now, (pair + 1, other[0]), (pair - 1, other[1]))

    def several(step, carry):
        pair = STAGES * step + 1
        chain(*[full(pair + n, (n + 1) % 2) for n in range(STAGES)])
        return carry

    chain(stage(None, (0, h1_even), None), stage(buffers[0], (1, h1_odd), None))
    steps = (pairs - 2) // STAGES
    lax.fori_loop(0, steps, several, 0)
    rest = [full(pair, pair % 2) for pair in range(STAGES * steps + 1, pairs - 1)]
    end = [last_job(h2_odd, n) for n in range(INNER // 2)], [last_done(pairs - 1)]
    chain(*rest, stage(buffers[1], None, (pairs - 2, h2_even)), end)

    lane = lax.broadcasted_iota(jnp.int32, (NT, NT), 0)
    time = lax.broadcasted_iota(jnp.int32, (NT, NT), 1)
    merge = one_hot(time == 2 * (lane % HALF) + lane // HALF)
    owners = sent_ref.shape[0]
    kept = BLK // owners

    def put(n, c, part):
        lanes = slice(n * UNIT, (n + 1) * UNIT)
        shot = slice(c * per_block, (c + 1) * per_block)
        denoised_ref[shot, :, lanes] = part.astype(BF16).reshape(per_block, RD, UNIT)
        rows4[:, c * kept : (c + 1) * kept, lanes] = part.reshape(owners, kept, UNIT)

    products(accs, [(cleaned[...].astype(BF16), merge, put)])
    sent_ref[:, :, :NT] = rows4[...].astype(BF16)
    shape = (sent_ref.shape[1], LANES)
    block = lax.broadcasted_iota(jnp.int32, shape, 0) // kept
    first_half = lax.broadcasted_iota(jnp.int32, shape, 1) < LANES // 2
    tag = jnp.zeros(shape, jnp.int32)
    for c in range(shots * RD // BLK):
        tag = jnp.where(block == c, jnp.where(first_half, target_ref[c], offset_ref[c]), tag)
    tag = tag.astype(F32).astype(BF16)
    sent_ref[:, :, NT:] = jnp.broadcast_to(tag[None], (owners, *shape))


def denoise_body(*refs):
    pl.run_scoped(
        lambda *accs: denoise_loop(*refs, (accs[: len(accs) // 2], accs[len(accs) // 2 :])),
        *[
            pltpu.ACC(unit)((BLK if number < 7 else 2 * RD, UNIT), F32)
            for unit in range(UNITS)
            for number in range(7 + INNER // 2)
        ],
    )


def denoise(offsets, targets, near, far, slots, first, middle, last, split):
    shots, blocks = slots.shape[0], offsets.shape[0]
    owners = lax.axis_size("tile")
    sent = (owners, blocks * BLK // owners, NT + LANES)
    scalars = pl.BlockSpec(memory_space=pltpu.SMEM)
    whole = pl.BlockSpec(memory_space=pltpu.VMEM)
    macs = shots * RD * NT * CH * (9 * CH + 18)
    return pl.pallas_call(
        denoise_body,
        out_shape=(pltpu.VMEM((shots, RD, NT), BF16), jax.ShapeDtypeStruct(sent, BF16)),
        in_specs=[scalars] * 2 + [whole] * 7,
        out_specs=(whole, whole),
        scratch_shapes=[pltpu.VMEM((HALF // LANES, shots * SIDE, LANES), F32)] * 2
        + [pltpu.VMEM((UNITS, OUTER, UNIT, HALF), BF16)] * 2
        + [pltpu.VMEM((UNITS, INNER * 2 * CH, HALF), BF16)] * 2
        + [pltpu.VMEM((shots * RD, NT), F32), pltpu.VMEM((*sent[:2], NT), F32)],
        compiler_params=pltpu.CompilerParams(vmem_limit_bytes=40 << 20),
        cost_estimate=pl.CostEstimate(flops=2 * macs, transcendentals=0, bytes_accessed=4 << 20),
        name="denoise",
    )(offsets, targets, near, far, slots, first, middle, last, split)


def stack_body(came_ref, map_ref, *part_refs):
    tiles, kept, _ = came_ref.shape
    rows = kept * BLK // (SH * RD)
    count = tiles * kept
    came = came_ref[...].reshape(count, NT + LANES)
    target = came[:, NT : NT + 1].astype(F32).astype(jnp.int32)
    offset = came[:, NT + LANES // 2 : NT + LANES // 2 + 1].astype(F32)
    traces = came[:, :NT]
    none = jnp.zeros_like(traces)
    wide = [jnp.where(offset == o, traces, none) for o in range(OB)]
    corrected = jnp.dot(
        jnp.concatenate(wide, axis=1), map_ref[...], preferred_element_type=F32
    )
    groups = len(part_refs)
    owned = MBLK // groups
    place = ((target // owned) ^ lax.axis_index("grp")) * owned + target % owned
    row = lax.broadcasted_iota(jnp.int32, (count, MBLK * rows), 0) % rows
    column = lax.broadcasted_iota(jnp.int32, (count, MBLK * rows), 1)
    chosen = one_hot((place == column // rows) & (row == column % rows))
    total = None
    for _ in range(3):
        part = corrected.astype(BF16)
        corrected = corrected - part.astype(F32)
        term = lax.dot_general(chosen, part, (((0,), (0,)), ((), ())), preferred_element_type=F32)
        total = term if total is None else total + term
    for number, ref in enumerate(part_refs):
        part = total[number * owned * rows : (number + 1) * owned * rows]
        ref[...] = part.reshape(ref.shape)


def stack(came, moveout_maps, groups):
    rows = came.shape[1] * BLK // (SH * RD)
    part = jax.ShapeDtypeStruct((MBLK // groups, rows, NT), F32)
    return pl.pallas_call(
        stack_body,
        out_shape=(part,) * groups,
        compiler_params=pltpu.CompilerParams(vmem_limit_bytes=40 << 20),
        name="stack",
    )(came, moveout_maps.reshape(OB * NT, NT))


def edges(own):
    odd = lax.axis_index("tile") % 2 == 1
    start, end = own[:, :EDGE, :].transpose(1, 0, 2), own[:, -EDGE:, :].transpose(1, 0, 2)
    return jnp.where(odd, start, end), jnp.where(odd, end, start)


def on_device(
    shot_data, weight_first, weight_middle, weight_last, moveout_maps, block_offset, block_target
):
    tiles, groups = lax.axis_size("tile"), lax.axis_size("grp")
    (own, weight_first, weight_middle, weight_last, block_offset, block_target) = (
        pltpu.with_memory_space_constraint(a, pltpu.HBM)
        for a in (
            shot_data,
            weight_first,
            weight_middle.reshape(9 * CH, CH),
            weight_last,
            block_offset,
            block_target.reshape(-1),
        )
    )
    near, far = edges(shot_data)
    near = lax.ppermute(near, "tile", [(i, i ^ 1) for i in range(tiles)])
    pairs = [(i, i + 1) for i in range(1, tiles - 1, 2)]
    far = lax.ppermute(far, "tile", pairs + [(j, i) for i, j in pairs])
    *weights, split, slots = prepare(weight_first, weight_middle, weight_last, own)
    denoised, sent = denoise(block_offset, block_target, near, far, slots, *weights, split)
    came = lax.all_to_all(sent, "tile", 0, 0, tiled=True)
    stacked, *parts = stack(came, moveout_maps, groups)
    for apart in (2, 1, 3):
        part = lax.ppermute(parts[apart - 1], "grp", [(g, g ^ apart) for g in range(groups)])
        stacked = stacked + part
    return denoised, stacked


def solution(mesh):
    in_specs = (
        P("grp", "tile", None),
        P(),
        P(),
        P(),
        P(),
        P(("grp", "tile")),
        P(("grp", "tile"), None),
    )
    out_specs = (P("grp", "tile", None), P("grp", "tile", None))
    return jax.shard_map(
        on_device, mesh=mesh, in_specs=in_specs, out_specs=out_specs, check_vma=False
    )
```

```python
import jax
import jax.numpy as jnp
from jax import lax
from jax.experimental import pallas as pl
from jax.experimental.pallas import tpu as pltpu
from jax.sharding import PartitionSpec as P

CH = 64
RD = 8
SH = 32
NT = 512
OB = 8
BLK = 128
MBLK = 32
LANES = 128
UNIT = 256
UNITS = 2
HALF = NT // 2
OUTER = RD + 4
INNER = RD + 2
EDGE = 3
SIDE = 16
STAGES = 6
F32 = jnp.float32
BF16 = jnp.bfloat16


def at_lane(shape, lane):
    return lax.broadcasted_iota(jnp.int32, shape, 1) % HALF == lane


def delayed(rows):
    return jnp.where(at_lane(rows.shape, 0), jnp.zeros_like(rows), pltpu.roll(rows, 1, 1))


def advanced(rows):
    last = rows.shape[1] - 1
    return jnp.where(at_lane(rows.shape, HALF - 1), jnp.zeros_like(rows), pltpu.roll(rows, last, 1))


def one_hot(condition):
    return condition.astype(F32).astype(BF16)


def prepare_body(tap1_ref, tap2_ref, tap3_ref, own_ref, first_ref, middle_ref, last_ref, split_ref, slots_ref, wide):
    tile = lax.axis_index("tile")
    low = (tile > 0).astype(F32)
    high = (tile < lax.axis_size("tile") - 1).astype(F32)

    shape = (9, UNIT)
    tap = lax.broadcasted_iota(jnp.int32, shape, 0)
    column = lax.broadcasted_iota(jnp.int32, shape, 1)
    inner = column - SIDE
    outer = inner - 4 * RD
    is_near, is_own = column < SIDE, inner < 4 * RD
    odd = tile % 2
    near, far = (EDGE + RD) * (1 - odd), (EDGE + RD) * odd
    across = jnp.where(is_near, column % 4 + near, jnp.where(is_own, inner % RD + EDGE, outer % 4 + far))
    delay = jnp.where(is_near, column // 4, jnp.where(is_own, inner // RD, outer // 4))
    used = (column < 2 * SIDE + 4 * RD) & ((is_near | (inner >= 4 * RD)) & (column % 4 < EDGE) | (inner >= 0) & is_own)
    for receiver in range(OUTER):
        inside = low if receiver < 2 else high if receiver >= OUTER - 2 else None
        for phase in range(2):
            a, d = across - receiver, delay - phase
            place = (tap == 3 * a + d) & (a >= 0) & (a <= 2) & (d >= 0) & (d <= 2) & used
            place = place.astype(F32)
            if inside is not None:
                place = place * inside
            block = lax.dot_general(
                tap1_ref[...], place.astype(BF16), (((0,), (0,)), ((), ())), preferred_element_type=F32
            )
            row = (2 * receiver + phase) * CH
            first_ref[row : row + CH, :] = block.astype(BF16)

    none = jnp.zeros((CH, CH), BF16)
    for across in range(3):
        taps = [tap2_ref[(3 * across + d) * CH : (3 * across + d + 1) * CH, :] for d in range(3)]
        lanes = slice(across * UNIT, (across + 1) * UNIT)
        middle_ref[:CH, lanes] = jnp.concatenate([*taps, none], axis=1)
        middle_ref[CH:, lanes] = jnp.concatenate([none, *taps], axis=1)

    none = jnp.zeros((1, CH), F32)
    taps = [tap3_ref[k : k + 1, :].astype(F32) for k in range(9)]
    kinds = [
        [taps[3 * a + 1] for a in range(3)], [taps[3 * a + 2] for a in range(3)],
        [taps[3 * a] for a in range(3)], [taps[3 * a + 1] for a in range(3)],
        [none] * 3, [taps[3 * a] for a in range(3)],
        [taps[3 * a + 2] for a in range(3)], [none] * 3,
    ]
    wide[...] = jnp.zeros_like(wide)
    for kind in range(4):
        row = [t for pair in zip(kinds[2 * kind], kinds[2 * kind + 1]) for t in pair]
        row = jnp.concatenate(row, axis=1)
        for receiver in range(RD):
            at = RD + receiver // 2 * RD + 2 * kind + receiver % 2
            wide[at : at + 1, receiver * 2 * CH : (receiver + 3) * 2 * CH] = row
    wide[:, : 2 * CH] = wide[:, : 2 * CH] * low
    wide[:, (INNER - 1) * 2 * CH :] = wide[:, (INNER - 1) * 2 * CH :] * high
    for n in range(INNER // 2):
        rows = slice(2 * n * RD, 2 * (n + 1) * RD)
        last_ref[rows, :] = wide[n * RD : (n + 2) * RD, n * UNIT : (n + 1) * UNIT].astype(BF16)

    time = lax.broadcasted_iota(jnp.int32, (NT, 4 * HALF), 0)
    lane = lax.broadcasted_iota(jnp.int32, (NT, 4 * HALF), 1)
    split = one_hot(time == 2 * (lane % HALF) + lane // HALF - 1)
    split_ref[...] = split
    shots = own_ref.shape[0]
    taken = jnp.dot(own_ref[...].reshape(shots * RD, NT), split, preferred_element_type=F32)
    parts = [taken[:, s * HALF : (s + 1) * HALF].reshape(shots, RD, HALF) for s in range(4)]
    slots_ref[...] = jnp.concatenate(parts, axis=1).astype(BF16)


def prepare(weight_first, weight_middle, weight_last, own):
    shapes = (
        (OUTER * 2 * CH, UNIT),
        (2 * CH, 3 * UNIT),
        (INNER * RD, UNIT),
        (NT, 4 * HALF),
        (own.shape[0], 4 * RD, HALF),
    )
    return pl.pallas_call(
        prepare_body,
        out_shape=tuple(jax.ShapeDtypeStruct(s, BF16) for s in shapes),
        scratch_shapes=[pltpu.VMEM(((INNER // 2 + 1) * RD, INNER * 2 * CH), F32)],
        compiler_params=pltpu.CompilerParams(vmem_limit_bytes=24 << 20),
        name="prepare",
    )(weight_first, weight_middle, weight_last, own)


def products(accs, items):
    taken = [0] * UNITS
    done = []
    for lhs, rhs, use in items:
        rows, depth = lhs.shape
        for n in range(rhs.shape[1] // UNIT):
            unit = n % UNITS
            held = accs[unit][taken[unit] : taken[unit] + rows // BLK]
            taken[unit] += len(held)
            for k in range(depth // UNIT):
                piece = rhs[k * UNIT : (k + 1) * UNIT, n * UNIT : (n + 1) * UNIT]
                pltpu.matmul_push_rhs(piece, k % 2, unit)
                for c, acc in enumerate(held):
                    piece = lhs[c * BLK : (c + 1) * BLK, k * UNIT : (k + 1) * UNIT]
                    pltpu.matmul_acc_lhs(acc, piece, load_staged_rhs=k % 2 if c == 0 else None)
            done += [(use, n, c, acc) for c, acc in enumerate(held)]
    for use, n, c, acc in done:
        use(n, c, pltpu.matmul_pop(acc))


def run(jobs):
    def push(number):
        for unit in range(UNITS):
            pltpu.matmul_push_rhs(jobs[number][0](unit), number % 2, unit)

    push(0)
    for number, (_, products, after) in enumerate(jobs):
        if number + 1 < len(jobs):
            push(number + 1)
        for n, (acc, lhs) in enumerate(products):
            for unit in range(UNITS):
                staged = number % 2 if n == 0 else None
                pltpu.matmul_acc_lhs(acc(unit), lhs(), load_staged_rhs=staged)
        for act in after:
            act()


def denoise_loop(
    offset_ref, target_ref, near_ref, far_ref, own, first_ref, middle_ref, last_ref, split_ref,
    denoised_ref, sent_ref, near, far, h1_even, h1_odd, h2_even, h2_odd, cleaned, rows4, accs,
):
    shots = own.shape[0]
    pairs = shots // UNITS
    per_block = BLK // RD

    items = []
    for ref, held in ((near_ref, near), (far_ref, far)):
        def keep(slot, c, part, held=held):
            for row in range(4):
                at = pl.ds(slot * 4 + row, shots, stride=SIDE)
                for half in range(HALF // LANES):
                    lanes = slice(half * LANES, (half + 1) * LANES)
                    held[half, at, :] = part[row * shots : (row + 1) * shots, lanes]

        edge = ref[...].reshape(EDGE * shots, NT)
        rest = jnp.zeros((BLK - EDGE * shots, NT), BF16)
        items.append((jnp.concatenate([edge, rest], axis=0), split_ref, keep))
    products(accs, items)

    def taps(pair):
        def right(unit):
            shot = pair * UNITS + unit
            rows = pl.ds(pl.multiple_of(shot * SIDE, SIDE), SIDE)
            rest = jnp.zeros((UNIT - 4 * RD - 2 * SIDE, HALF), BF16)
            sides = [
                jnp.concatenate([side[0, rows, :], side[1, rows, :]], axis=1).astype(BF16)
                for side in (near, far)
            ]
            return jnp.concatenate([sides[0], own[shot], sides[1], rest], axis=0)

        return right

    def first_done(h1, receiver):
        def act():
            for unit in range(UNITS):
                both = jnp.maximum(pltpu.matmul_pop(accs[unit][receiver % 3]), 0.0).astype(BF16)
                h1[unit, receiver, CH : 3 * CH, :] = both
                h1[unit, receiver, :CH, :] = delayed(both[CH:])
                h1[unit, receiver, 3 * CH :, :] = advanced(both[:CH])

        return act

    def middle_done(h2, receiver):
        def act():
            for unit in range(UNITS):
                both = jnp.maximum(pltpu.matmul_pop(accs[unit][3 + receiver % 4]), 0.0)
                h2[unit, receiver * 2 * CH : (receiver + 1) * 2 * CH, :] = both.astype(BF16)

        return act

    def last_done(pair):
        def act():
            for unit in range(UNITS):
                shot = pair * UNITS + unit
                parts = [pltpu.matmul_pop(acc) for acc in accs[unit][7:]]
                sums = [low[RD:] + high[:RD] for low, high in zip(parts, parts[1:])]
                kinds = [jnp.concatenate([p[2 * k : 2 * k + 2] for p in sums], axis=0) for k in range(4)]
                seen = own[shot].astype(F32)
                rows = pl.ds(pl.multiple_of(shot * RD, RD), RD)
                even = kinds[0] + delayed(kinds[2])
                odd = kinds[1] + advanced(kinds[3])
                cleaned[rows, :HALF] = seen[RD : 2 * RD] - even
                cleaned[rows, HALF:] = seen[2 * RD : 3 * RD] - odd

        return act

    def first_job(pair, receivers):
        products = [
            (
                lambda unit, r=r: accs[unit][r % 3],
                lambda r=r: first_ref[r * 2 * CH : (r + 1) * 2 * CH, :],
            )
            for r in receivers
        ]
        return taps(pair), products, []

    def middle_job(h1, receiver):
        products = [
            (
                lambda unit, r=receiver - across: accs[unit][3 + r % 4],
                lambda across=across: middle_ref[:, across * UNIT : (across + 1) * UNIT],
            )
            for across in (2, 1, 0)
            if 0 <= receiver - across < INNER
        ]
        return lambda unit: h1[unit, receiver], products, []

    def last_job(h2, number):
        lanes = slice(number * UNIT, (number + 1) * UNIT)
        rows = slice(2 * number * RD, 2 * (number + 1) * RD)
        products = [(lambda unit: accs[unit][7 + number], lambda: last_ref[rows, :])]
        return lambda unit: h2[unit, lanes, :], products, []

    def stage(now, later, before):
        jobs = []
        for r in range(OUTER):
            if later and r % 3 == 0:
                jobs.append(first_job(later[0], range(r, r + 3)))
            if now:
                jobs.append(middle_job(now[0], r))
            if later:
                jobs[-1][2].append(first_done(later[1], r))
            if now and r >= 3:
                jobs[-1][2].append(middle_done(now[1], r - 3))
            if before and r % 2 == 1 and r < INNER:
                jobs.append(last_job(before[1], r // 2))
            if before and r == INNER:
                jobs[-1][2].append(last_done(before[0]))
        return jobs, [middle_done(now[1], INNER - 1)] if now else []

    def chain(*stages):
        jobs, tail = [], []
        for more, end in stages:
            more[0][2].extend(tail)
            jobs, tail = jobs + more, end
        jobs[-1][2].extend(tail)
        run(jobs)

    buffers = ((h1_even, h2_even), (h1_odd, h2_odd))

    def full(pair, parity):
        now, other = buffers[parity], buffers[1 - parity]
        return stage(now, (pair + 1, other[0]), (pair - 1, other[1]))

    def several(step, carry):
        pair = STAGES * step + 1
        chain(*[full(pair + n, (n + 1) % 2) for n in range(STAGES)])
        return carry

    chain(stage(None, (0, h1_even), None), stage(buffers[0], (1, h1_odd), None))
    steps = (pairs - 2) // STAGES
    lax.fori_loop(0, steps, several, 0)
    rest = [full(pair, pair % 2) for pair in range(STAGES * steps + 1, pairs - 1)]
    end = [last_job(h2_odd, n) for n in range(INNER // 2)], [last_done(pairs - 1)]
    chain(*rest, stage(buffers[1], None, (pairs - 2, h2_even)), end)

    lane = lax.broadcasted_iota(jnp.int32, (NT, NT), 0)
    time = lax.broadcasted_iota(jnp.int32, (NT, NT), 1)
    merge = one_hot(time == 2 * (lane % HALF) + lane // HALF)
    owners = sent_ref.shape[0]
    kept = BLK // owners

    def put(n, c, part):
        lanes = slice(n * UNIT, (n + 1) * UNIT)
        shot = slice(c * per_block, (c + 1) * per_block)
        denoised_ref[shot, :, lanes] = part.astype(BF16).reshape(per_block, RD, UNIT)
        rows4[:, c * kept : (c + 1) * kept, lanes] = part.reshape(owners, kept, UNIT)

    products(accs, [(cleaned[...].astype(BF16), merge, put)])
    sent_ref[:, :, :NT] = rows4[...].astype(BF16)
    shape = (sent_ref.shape[1], LANES)
    block = lax.broadcasted_iota(jnp.int32, shape, 0) // kept
    first_half = lax.broadcasted_iota(jnp.int32, shape, 1) < LANES // 2
    tag = jnp.zeros(shape, jnp.int32)
    for c in range(shots * RD // BLK):
        tag = jnp.where(block == c, jnp.where(first_half, target_ref[c], offset_ref[c]), tag)
    tag = tag.astype(F32).astype(BF16)
    sent_ref[:, :, NT:] = jnp.broadcast_to(tag[None], (owners, *shape))


def denoise_body(*refs):
    pl.run_scoped(
        lambda *accs: denoise_loop(*refs, (accs[: len(accs) // 2], accs[len(accs) // 2 :])),
        *[
            pltpu.ACC(unit)((BLK if number < 7 else 2 * RD, UNIT), F32)
            for unit in range(UNITS)
            for number in range(7 + INNER // 2)
        ],
    )


def denoise(offsets, targets, near, far, slots, first, middle, last, split):
    shots, blocks = slots.shape[0], offsets.shape[0]
    owners = lax.axis_size("tile")
    sent = (owners, blocks * BLK // owners, NT + LANES)
    scalars = pl.BlockSpec(memory_space=pltpu.SMEM)
    whole = pl.BlockSpec(memory_space=pltpu.VMEM)
    macs = shots * RD * NT * CH * (9 * CH + 18)
    return pl.pallas_call(
        denoise_body,
        out_shape=(pltpu.VMEM((shots, RD, NT), BF16), jax.ShapeDtypeStruct(sent, BF16)),
        in_specs=[scalars] * 2 + [whole] * 7,
        out_specs=(whole, whole),
        scratch_shapes=[pltpu.VMEM((HALF // LANES, shots * SIDE, LANES), F32)] * 2
        + [pltpu.VMEM((UNITS, OUTER, UNIT, HALF), BF16)] * 2
        + [pltpu.VMEM((UNITS, INNER * 2 * CH, HALF), BF16)] * 2
        + [pltpu.VMEM((shots * RD, NT), F32), pltpu.VMEM((*sent[:2], NT), F32)],
        compiler_params=pltpu.CompilerParams(vmem_limit_bytes=40 << 20),
        cost_estimate=pl.CostEstimate(flops=2 * macs, transcendentals=0, bytes_accessed=4 << 20),
        name="denoise",
    )(offsets, targets, near, far, slots, first, middle, last, split)


def stack_body(came_ref, map_ref, *part_refs):
    tiles, kept, _ = came_ref.shape
    rows = kept * BLK // (SH * RD)
    count = tiles * kept
    came = came_ref[...].reshape(count, NT + LANES)
    target = came[:, NT : NT + 1].astype(F32).astype(jnp.int32)
    offset = came[:, NT + LANES // 2 : NT + LANES // 2 + 1].astype(F32)
    traces = came[:, :NT]
    none = jnp.zeros_like(traces)
    wide = [jnp.where(offset == o, traces, none) for o in range(OB)]
    corrected = jnp.dot(
        jnp.concatenate(wide, axis=1), map_ref[...], preferred_element_type=F32
    )
    groups = len(part_refs)
    owned = MBLK // groups
    place = ((target // owned) ^ lax.axis_index("grp")) * owned + target % owned
    row = lax.broadcasted_iota(jnp.int32, (count, MBLK * rows), 0) % rows
    column = lax.broadcasted_iota(jnp.int32, (count, MBLK * rows), 1)
    chosen = one_hot((place == column // rows) & (row == column % rows))
    total = None
    for _ in range(3):
        part = corrected.astype(BF16)
        corrected = corrected - part.astype(F32)
        term = lax.dot_general(chosen, part, (((0,), (0,)), ((), ())), preferred_element_type=F32)
        total = term if total is None else total + term
    for number, ref in enumerate(part_refs):
        part = total[number * owned * rows : (number + 1) * owned * rows]
        ref[...] = part.reshape(ref.shape)


def stack(came, moveout_maps, groups):
    rows = came.shape[1] * BLK // (SH * RD)
    part = jax.ShapeDtypeStruct((MBLK // groups, rows, NT), F32)
    return pl.pallas_call(
        stack_body,
        out_shape=(part,) * groups,
        compiler_params=pltpu.CompilerParams(vmem_limit_bytes=40 << 20),
        name="stack",
    )(came, moveout_maps.reshape(OB * NT, NT))


def edges(own):
    odd = lax.axis_index("tile") % 2 == 1
    start, end = own[:, :EDGE, :].transpose(1, 0, 2), own[:, -EDGE:, :].transpose(1, 0, 2)
    return jnp.where(odd, start, end), jnp.where(odd, end, start)


def on_device(
    shot_data, weight_first, weight_middle, weight_last, moveout_maps, block_offset, block_target
):
    tiles, groups = lax.axis_size("tile"), lax.axis_size("grp")
    (own, weight_first, weight_middle, weight_last, block_offset, block_target) = (
        pltpu.with_memory_space_constraint(a, pltpu.HBM)
        for a in (
            shot_data,
            weight_first,
            weight_middle.reshape(9 * CH, CH),
            weight_last,
            block_offset,
            block_target.reshape(-1),
        )
    )
    near, far = edges(shot_data)
    near = lax.ppermute(near, "tile", [(i, i ^ 1) for i in range(tiles)])
    pairs = [(i, i + 1) for i in range(1, tiles - 1, 2)]
    far = lax.ppermute(far, "tile", pairs + [(j, i) for i, j in pairs])
    *weights, split, slots = prepare(weight_first, weight_middle, weight_last, own)
    denoised, sent = denoise(block_offset, block_target, near, far, slots, *weights, split)
    came = lax.all_to_all(sent, "tile", 0, 0, tiled=True)
    stacked, *parts = stack(came, moveout_maps, groups)
    for apart in (2, 1, 3):
        part = lax.ppermute(parts[apart - 1], "grp", [(g, g ^ apart) for g in range(groups)])
        stacked = stacked + part
    return denoised, stacked


def solution(mesh):
    in_specs = (
        P("grp", "tile", None),
        P(),
        P(),
        P(),
        P(),
        P(("grp", "tile")),
        P(("grp", "tile"), None),
    )
    out_specs = (P("grp", "tile", None), P("grp", "tile", None))
    return jax.shard_map(
        on_device, mesh=mesh, in_specs=in_specs, out_specs=out_specs, check_vma=False
    )
```
